512 devices in a mesh: gx: 128 (over y, x_hi, z), gz: 4 (over x_lo, core).
Axes of the slice: x: 4 (x_hi: 2, x_lo: 2; x = x_hi * 2 + x_lo), y: 4, z: 16, core: 2. Of those that a mesh axis runs over, the one named last changes fastest.
Arguments:
- pressure: float32 [64, 2048, 256], P('gz', 'gx'), may hold values from -6 to 6
- saturation: float32 [64, 2048, 256], P('gz', 'gx'), may hold values from 0.05 to 0.8
- sat_history: float32 [64, 2048, 256], P('gz', 'gx'), may hold values from 0.05 to 0.85, as said below
- storage: float32 [64, 2048, 256], P('gz', 'gx'), may hold values from 0.3 to 3
- step_volume: float32 [64, 2048, 256], P('gz', 'gx'), may hold values from 0.005 to 0.05
- transmiss: float32 [3, 64, 2048, 256], P(None, 'gz', 'gx'), may hold values from 0.1 to 2
- perf_cell: int32 [4096, 16], P('gx'), may hold values from 0 to 262143, as said below
- perf_index: float32 [4096, 16], P('gx'), may hold values from 0.2 to 2
- control: int32 [4096], P('gx'), may hold values from 0 to 1
- target: float32 [4096], P('gx'), may hold values from 0.5 to 3
Outputs:
- new_pressure: float32 [64, 2048, 256], P('gz', 'gx')
- residual: float32 [64, 2048, 256], P('gz', 'gx')
- new_saturation: float32 [64, 2048, 256], P('gz', 'gx')
- new_history: float32 [64, 2048, 256], P('gz', 'gx')
- bottom_hole: float32 [4096], P('gx')
The draws below stay inside these ranges and needn't reach their ends.
Inputs may be any that keep to these rules, and one draw needn't show every extreme that they name: `perf_cell`: each perforation number names a cell of its own well's row of tiles, counted as layer * 16 * 256 + first lateral index within the row * 256 + second lateral index; a well's perforations lie in 16 consecutive layers, one a layer, top first, and from one to the next each lateral index moves by at most one cell. sat_history is at least the cell's saturation.
All inputs are finite; a program needn't handle non-finite values.
Results may differ from the reference program's by a relative error of at most 0.0003.
Values sent between devices are 32-bit elements; how exact they have to be, the bound alone decides.
A program may use at most 64 MiB of HBM per device.

```python
import math
import jax
import jax.numpy as jnp
from jax import lax

CX = 16
NY = 256
WELL_ROW = 32
NPERF = 16
SWEEPS = 4
NZ = 64
NX = 2048
NWELL = 4096


def joint_saturation(key):
    base = jax.random.fold_in(key, 11)
    first, second, third = jax.random.split(base, 3)
    shape = (NZ, NX, NY)
    sat = jax.random.uniform(first, shape, jnp.float32, 0.05, 0.8)
    increment = jax.random.uniform(second, shape, jnp.float32, 0.0, 0.4)
    keep = jax.random.uniform(third, shape, jnp.float32) < 0.3
    history = jnp.minimum(sat + jnp.where(keep, 0.0, increment), 0.85)
    return (sat, history)


def draw_saturation(key, part):
    return joint_saturation(key)[0]


def draw_sat_history(key, part):
    return joint_saturation(key)[1]


def draw_perf_cell(key, part):
    base = jax.random.fold_in(key, 23)
    keys = jax.random.split(base, 5)
    top = jax.random.randint(keys[0], (NWELL, 1), 0, NZ - NPERF + 1)
    lateral_head = jax.random.randint(keys[1], (NWELL, 1), 0, CX)
    column_head = jax.random.randint(keys[2], (NWELL, 1), 0, NY)
    first_col = jnp.arange(NPERF, dtype=jnp.int32)[None, :] == 0
    lateral_step = jnp.where(first_col, 0, jax.random.randint(keys[3], (NWELL, NPERF), -1, 2))
    column_step = jnp.where(first_col, 0, jax.random.randint(keys[4], (NWELL, NPERF), -1, 2))
    lateral = jnp.clip(lateral_head + jnp.cumsum(lateral_step, axis=1), 0, CX - 1)
    column = jnp.clip(column_head + jnp.cumsum(column_step, axis=1), 0, NY - 1)
    layer = top + jnp.arange(NPERF, dtype=jnp.int32)[None, :]
    return (layer * (CX * NY) + lateral * NY + column).astype(jnp.int32)


def set_ends(values, stream_key, low, high):
    longest = values.shape.index(max(values.shape))
    spots = []
    for shift in (0, 1):
        where = [jax.random.randint(jax.random.fold_in(stream_key, axis), (), 0, length) for axis, length in enumerate(values.shape)]
        where[longest] = (where[longest] + shift) % values.shape[longest]
        spots.append(tuple(where))
    return values.at[spots[0]].set(low).at[spots[1]].set(high)


def levels(own_key, shape, pieces, least, high):
    def one(dim, parts):
        heights = jax.random.uniform(jax.random.fold_in(jax.random.fold_in(own_key, 6), dim), (parts,), jnp.float32, least / len(pieces), high / len(pieces))
        return jnp.repeat(jnp.exp(heights), shape[dim] // parts).reshape((-1,) + (1,) * (len(shape) - dim - 1))

    level = one(*pieces[0])
    for cut in pieces[1:]:
        level = level * one(*cut)
    return level


def scatter_about(key, extent, scale, bound, cuts=(), kind=jnp.bfloat16):
    factor_of = levels(key, extent, cuts, -0.22, 0.18) if cuts else 1.0
    array = jax.random.normal(key, extent, jnp.float32) * scale * factor_of
    return jnp.minimum(jnp.maximum(array, -bound), bound).astype(kind)


def setup_inputs(seed: int = 0) -> dict:
    splits = jax.random.split(jax.random.key(seed), 11)
    return {
        "pressure": scatter_about(splits[0], (NZ, NX, NY), 1.0, 6.0, ((0, 4), (1, 128)), jnp.float32),
        "saturation": draw_saturation(jax.random.fold_in(splits[10], 71), 0),
        "sat_history": draw_sat_history(jax.random.fold_in(splits[10], 71), 0),
        "storage": jnp.clip(jnp.exp(math.log(3.0) - 2.3025851 * jax.random.uniform(splits[3], (NZ, NX, NY), jnp.float32) ** levels(splits[3], (NZ, NX, NY), ((0, 4), (1, 128)), -0.2, 0.2)), 0.3, 3.0),
        "step_volume": jnp.clip(jnp.exp(math.log(0.05) - 2.3025851 * jax.random.uniform(splits[4], (NZ, NX, NY), jnp.float32) ** levels(splits[4], (NZ, NX, NY), ((0, 4), (1, 128)), -0.2, 0.2)), 0.005, 0.05),
        "transmiss": jnp.clip(jnp.exp(math.log(2.0) - 2.9957323 * jax.random.uniform(splits[5], (3, NZ, NX, NY), jnp.float32) ** levels(splits[5], (3, NZ, NX, NY), ((1, 4), (2, 128)), -0.2, 0.2)), 0.1, 2.0),
        "perf_cell": draw_perf_cell(jax.random.fold_in(splits[10], 71), 0),
        "perf_index": jnp.clip(jnp.exp(math.log(2.0) - 2.3025851 * jax.random.uniform(splits[7], (NWELL, NPERF), jnp.float32) ** levels(splits[7], (NWELL, NPERF), ((0, 128),), -0.2, 0.2)), 0.2, 2.0),
        "control": set_ends(jax.random.randint(splits[8], (NWELL,), 0, 2), jax.random.fold_in(splits[8], 1), 0, 1).astype(jnp.int32),
        "target": jnp.clip(0.5 + 2.5 * jax.random.uniform(splits[9], (NWELL,), jnp.float32) ** levels(splits[9], (NWELL,), ((0, 128),), -0.2, 0.2), 0.5, 3.0),
    }


def mobility(sat, history):
    trapped = history / (1.0 + 1.5 * history)
    excess = jnp.maximum(sat - trapped, 0.0)
    free_gas = 0.5 * (excess + jnp.sqrt(excess * excess + excess / 0.375))
    relperm = jnp.where(sat < history, free_gas * free_gas, sat * sat)
    gas = relperm / 0.5
    total = (1.0 - sat) * (1.0 - sat) + gas
    return (total, gas / total)

def next_cell(field, axis):
    size = field.shape[axis]
    tail = jnp.zeros_like(lax.slice_in_dim(field, 0, 1, axis=axis))
    return jnp.concatenate([lax.slice_in_dim(field, 1, size, axis=axis), tail], axis=axis)

def prev_cell(field, axis):
    size = field.shape[axis]
    head = jnp.zeros_like(lax.slice_in_dim(field, 0, 1, axis=axis))
    return jnp.concatenate([head, lax.slice_in_dim(field, 0, size - 1, axis=axis)], axis=axis)

def face_terms(transmiss, total):
    terms = []
    for axis in range(3):
        faces = transmiss[axis]
        index = lax.broadcasted_iota(jnp.int32, faces.shape, axis)
        plus_t = jnp.where(index < faces.shape[axis] - 1, faces, 0.0)
        minus_t = prev_cell(faces, axis)
        plus = plus_t * 0.5 * (total + next_cell(total, axis))
        minus = minus_t * 0.5 * (total + prev_cell(total, axis))
        terms.append((plus, minus))
    return terms

def operate(field, storage, terms):
    result = storage * field
    for axis in range(3):
        plus, minus = terms[axis]
        result = result + plus * (field - next_cell(field, axis)) + minus * (field - prev_cell(field, axis))
    return result

def reference(pressure, saturation, sat_history, storage, step_volume, transmiss, perf_cell, perf_index, control, target):
    total, frac = mobility(saturation, sat_history)
    terms = face_terms(transmiss, total)
    diag = storage
    for axis in range(3):
        diag = diag + terms[axis][0] + terms[axis][1]
    row_id = (jnp.arange(NWELL, dtype=jnp.int32) // WELL_ROW)[:, None]
    layer = perf_cell // (CX * NY)
    rest = perf_cell % (CX * NY)
    lateral = row_id * CX + rest // NY
    column = rest % NY
    weight = perf_index * total[layer, lateral, column]
    cell_p = pressure[layer, lateral, column]
    sum_p = lax.optimization_barrier(jnp.sum(weight * cell_p, axis=1))
    sum_w = lax.optimization_barrier(jnp.sum(weight, axis=1))
    bottom_hole = jnp.where(control == 0, (target + sum_p) / sum_w, target)
    rate = weight * (bottom_hole[:, None] - cell_p)
    source = jnp.zeros(pressure.shape, jnp.float32).at[layer, lateral, column].add(rate)
    rhs = storage * pressure + source
    field = pressure
    for sweep in range(SWEEPS):
        field = field + (rhs - operate(field, storage, terms)) / diag
    residual = rhs - operate(field, storage, terms)
    out = jnp.zeros_like(field)
    for axis in range(3):
        plus, minus = terms[axis]
        flow_up = plus * (field - next_cell(field, axis))
        out = out + flow_up * jnp.where(flow_up > 0, frac, next_cell(frac, axis))
        flow_down = minus * (field - prev_cell(field, axis))
        out = out + flow_down * jnp.where(flow_down > 0, frac, prev_cell(frac, axis))
    gas_source = jnp.maximum(source, 0.0) + jnp.minimum(source, 0.0) * frac
    new_saturation = saturation + step_volume * (gas_source - out)
    new_history = jnp.maximum(sat_history, new_saturation)
    return (field, residual, new_saturation, new_history, bottom_hole)
```

```python
import functools

import jax
import jax.numpy as jnp
from jax import lax
from jax.experimental import pallas as pl
from jax.experimental.pallas import tpu as pltpu
from jax.sharding import PartitionSpec as P

L = 16
R = 16
C = 256
H = 4
X = L + 2 * H
WELLS = 32
NP = 16
GROUPS = WELLS * NP // 128
HI = L
LO = L + H
AP, ATO, AST, AT0, AT1, AT2 = range(6)
PACKED = (AP, AST, AT0, AT1, AT2)
RAW = 4 * len(PACKED)
PAIRS = ((AP, ATO), (AST, AT0), (AT1, AT2))
MESH = pl.DeviceIdType.MESH
F32 = jnp.float32
BF16 = jnp.bfloat16
VMEM_LIMIT = 26 * 2**20


def mobility(sat, history):
    trapped = history / (1.0 + 1.5 * history)
    excess = jnp.maximum(sat - trapped, 0.0)
    free_gas = 0.5 * (excess + jnp.sqrt(excess * excess + excess / 0.375))
    relperm = jnp.where(sat < history, free_gas * free_gas, sat * sat)
    gas = relperm / 0.5
    total = (1.0 - sat) * (1.0 - sat) + gas
    return (total, gas / total)


def split(values):
    high = values.astype(BF16)
    low = (values - high.astype(F32)).astype(BF16)
    return high, low


def four(row):
    return jnp.concatenate([row, row, row, row], axis=1)


def lane_groups(table):
    wide = four(table)
    place = lax.broadcasted_iota(jnp.int32, (1, 128), 1) // WELLS
    rows = []
    for g in range(GROUPS):
        row = wide[4 * g : 4 * g + 1]
        for k in range(1, 4):
            row = jnp.where(place == k, wide[4 * g + k : 4 * g + k + 1], row)
        rows.append(row)
    return rows


def cell_parts(cell, gz):
    layer = lax.shift_right_logical(cell, 12) - gz * L
    row = lax.shift_right_logical(cell, 8) & (R - 1)
    column = cell & (C - 1)
    index = jnp.where(layer < 0, layer + X, layer)
    inside = (layer >= -H) & (layer < L + H)
    return index, row, column, inside


def one_hot(size, target):
    return jnp.where(lax.broadcasted_iota(jnp.int32, (size, 128), 0) == target, 1.0, 0.0)


def own_rows(cell, gz):
    index, row, _, inside = cell_parts(cell, gz)
    return jnp.where(inside, index * R + row, -1)


def side_rows(cell, gz, side):
    index, row, _, inside = cell_parts(cell, gz)
    if side == 0:
        inside = inside & (row >= R - H)
        place = index * 8 + row - 8
    else:
        inside = inside & (row < H)
        place = index * 8 + row
    return jnp.where(inside, place, -1)


def scatter(rows, values):
    high, low = split(values)
    dims = (((1,), (1,)), ((), ()))
    return lax.dot_general(rows, high, dims, preferred_element_type=F32) + lax.dot_general(
        rows, low, dims, preferred_element_type=F32
    )


def column_values(columns, values):
    place = lax.broadcasted_iota(jnp.int32, (C, 128), 0)
    return jnp.concatenate(
        [jnp.where(place == c, v, 0.0) for c, v in zip(columns, values)], axis=1
    )


def exchange(
    count_x,
    count_z,
    p_in,
    sat_in,
    hist_in,
    sto_in,
    vol_in,
    tr_in,
    pc_in,
    pi_in,
    ctl_in,
    tgt_in,
    ext,
    frac,
    local,
    index_sum,
    own_hot,
    side_hot,
    cols,
    idxs,
    edge_x,
    edge_z,
    tiles,
    raw_out,
    raw_in,
    cmp_out,
    cmp_in,
    corner_out,
    corner_in,
    edge_out,
    tile_out,
    pc,
    pi,
    ctl,
    tgt,
    load_sem,
    send_sem,
    recv_sem,
):
    gx, gz = lax.axis_index("gx"), lax.axis_index("gz")
    has = {
        ("x", 0): gx > 0,
        ("x", 1): gx < count_x - 1,
        ("z", 0): gz > 0,
        ("z", 1): gz < count_z - 1,
    }
    step = (-1, 1)

    barrier = pltpu.get_barrier_semaphore()

    def signal_column(x):
        def one(z, carry):
            pl.semaphore_signal(barrier, inc=1, device_id=(x, z), device_id_type=MESH)
            return carry

        return one

    def others(z, carry):
        @pl.when(z != gz)
        def _():
            pl.semaphore_signal(barrier, inc=1, device_id=(gx, z), device_id_type=MESH)

        return carry

    for s in (0, 1):

        @pl.when(has["x", s])
        def _():
            lax.fori_loop(0, count_z, signal_column(gx + step[s]), 0)

    lax.fori_loop(0, count_z, others, 0)

    own = pl.ds(0, L)
    loads = [
        pltpu.make_async_copy(pc_in, pc.at[0], load_sem.at[0]),
        pltpu.make_async_copy(pi_in, pi.at[0], load_sem.at[1]),
        pltpu.make_async_copy(ctl_in, ctl, load_sem.at[2]),
        pltpu.make_async_copy(tgt_in, tgt, load_sem.at[3]),
        pltpu.make_async_copy(p_in, ext.at[AP, own, own], load_sem.at[4]),
        pltpu.make_async_copy(sto_in, ext.at[AST, own, own], load_sem.at[5]),
        pltpu.make_async_copy(tr_in, ext.at[pl.ds(AT0, 3), own, own], load_sem.at[6]),
        pltpu.make_async_copy(sat_in, local.at[0], load_sem.at[7]),
        pltpu.make_async_copy(hist_in, local.at[1], load_sem.at[8]),
        pltpu.make_async_copy(vol_in, local.at[2], load_sem.at[9]),
    ]
    for copy in loads:
        copy.start()

    for s in (0, 1):
        z0 = LO if s == 0 else HI

        @pl.when(jnp.logical_not(has["x", s]))
        def _():
            raw_in[s] = jnp.zeros((RAW, L, C), F32)
            raw_in[s, 4:8] = jnp.ones((4, L, C), F32)
            cmp_in[s] = jnp.zeros((5, L, C), F32)
            edge_x[s] = jnp.zeros((2, L, C), F32)
            pc[1 + s] = jnp.full((NP, WELLS), 1 << 30, jnp.int32)
            pi[1 + s] = jnp.zeros((NP, WELLS), F32)
            tiles[4 * (2 * s) : 4 * (2 * s) + 4] = jnp.ones((4, 8, 128), F32)

        @pl.when(jnp.logical_not(has["z", s]))
        def _():
            for a in range(6):
                fill = jnp.ones if a == AST else jnp.zeros
                ext[a, z0 : z0 + H, 0:R, :] = fill((H, R, C), F32)
            frac[X - 1 if s == 0 else HI, 0:R, :] = jnp.zeros((R, C), F32)
            edge_z[s] = jnp.zeros((2, R, C), F32)

        for t in (0, 1):

            @pl.when(jnp.logical_not(has["x", s] & has["z", t]))
            def _():
                c = 2 * s + t
                corner_in[c] = jnp.zeros((12, 8, C), F32)
                corner_in[c, 4:8, 0:4] = jnp.ones((4, 4, C), F32)

    for n in (4, 5, 6):
        loads[n].wait()
    for s, base in ((0, R - H), (1, 0)):
        for n, a in enumerate(PACKED):
            for i in range(H):
                raw_out[s, 4 * n + i] = ext[a, 0:L, base + i, :]

    pl.semaphore_wait(
        barrier,
        count_z * (1 + has["x", 0].astype(jnp.int32) + has["x", 1].astype(jnp.int32)) - 1,
    )

    def remote(src, dst, sem, device):
        return pltpu.make_async_remote_copy(
            src_ref=src,
            dst_ref=dst,
            send_sem=send_sem.at[sem],
            recv_sem=recv_sem.at[sem],
            device_id=device,
            device_id_type=MESH,
        )

    early, late = [], []
    for s in (0, 1):
        to_x = (gx + 1, gz) if s == 0 else (gx - 1, gz)
        to_z = (gx, gz + 1) if s == 0 else (gx, gz - 1)
        out_x, out_z = has["x", 1 - s], has["z", 1 - s]
        src_l = pl.ds(L - H if s == 0 else 0, H)
        dst_l = pl.ds(LO if s == 0 else HI, H)
        b = 12 * s
        early += [
            (out_x, has["x", s], remote(pc_in, pc.at[1 + s], b + 0, to_x)),
            (out_x, has["x", s], remote(pi_in, pi.at[1 + s], b + 1, to_x)),
            (out_x, has["x", s], remote(raw_out.at[s], raw_in.at[s], b + 2, to_x)),
            (out_z, has["z", s], remote(p_in.at[src_l], ext.at[AP, dst_l, own], b + 3, to_z)),
            (out_z, has["z", s], remote(sto_in.at[src_l], ext.at[AST, dst_l, own], b + 4, to_z)),
            (
                out_z,
                has["z", s],
                remote(tr_in.at[:, src_l], ext.at[pl.ds(AT0, 3), dst_l, own], b + 5, to_z),
            ),
        ]
        late += [
            (out_x, has["x", s], remote(cmp_out.at[s, pl.ds(0, 5)], cmp_in.at[s], b + 6, to_x)),
            (out_x, has["x", s], remote(cmp_out.at[s, pl.ds(5, 2)], edge_x.at[s], b + 7, to_x)),
            (
                out_z,
                has["z", s],
                remote(ext.at[ATO, src_l, own], ext.at[ATO, dst_l, own], b + 8, to_z),
            ),
            (
                out_z,
                has["z", s],
                remote(
                    frac.at[pl.ds(L - 1 if s == 0 else 0, 1), own],
                    frac.at[pl.ds(X - 1 if s == 0 else HI, 1), own],
                    b + 9,
                    to_z,
                ),
            ),
            (out_z, has["z", s], remote(edge_out.at[s], edge_z.at[s], b + 10, to_z)),
        ]
        for t in (0, 1):
            c = 2 * s + t
            to = (to_x[0], gz + 1 if t == 0 else gz - 1)
            late.append(
                (
                    out_x & has["z", 1 - t],
                    has["x", s] & has["z", t],
                    remote(corner_out.at[c], corner_in.at[c], 24 + c, to),
                )
            )

    def start(copies):
        for out, _, copy in copies:

            @pl.when(out)
            def _():
                copy.start()

    start(early)

    for n in (7, 8):
        loads[n].wait()
    for l in range(L):
        total, fraction = mobility(local[0, l], local[1, l])
        ext[ATO, l, 0:R, :] = total
        frac[l, 0:R, :] = fraction

    for s, base in ((0, R - H), (1, 0)):
        for i in range(H):
            cmp_out[s, i] = ext[ATO, 0:L, base + i, :]
        cmp_out[s, 4] = frac[0:L, R - 1 if s == 0 else 0, :]
        inner, outer = (R - H, R - H - 1) if s == 0 else (H - 1, H)
        face = R - H - 1 if s == 0 else H - 1
        rate = (
            ext[AT1, 0:L, face, :]
            * 0.5
            * (ext[ATO, 0:L, inner, :] + ext[ATO, 0:L, outer, :])
        )
        cmp_out[s, 5] = rate
        cmp_out[s, 6] = rate * ext[AP, 0:L, outer, :]
        rate = ext[AT0, face, 0:R, :] * 0.5 * (ext[ATO, inner, 0:R, :] + ext[ATO, outer, 0:R, :])
        edge_out[s, 0] = rate
        edge_out[s, 1] = rate * ext[AP, outer, 0:R, :]
        for t in (0, 1):
            l0 = L - H if t == 0 else 0
            for n, pair in enumerate(PAIRS):
                for i in range(H):
                    for h, a in enumerate(pair):
                        corner_out[2 * s + t, 4 * n + i, 4 * h : 4 * h + 4, :] = ext[
                            a, l0 : l0 + H, base + i, :
                        ]
    start(late)

    for n in (0, 1, 2, 3):
        loads[n].wait()
    cell = lane_groups(pc[0])
    index = lane_groups(pi[0])
    column = [cell_parts(v, gz)[2] for v in cell]
    rows = [one_hot(X * R, own_rows(v, gz)) for v in cell]
    for g in range(GROUPS):
        own_hot[:, 128 * g : 128 * g + 128] = rows[g].astype(BF16)
        cols[0, g : g + 1] = column[g]
        idxs[0, g : g + 1] = index[g]
    hot = jnp.concatenate([one_hot(C, c).astype(BF16) for c in column], axis=1)
    field = ext[ATO, 0:L, 0:R, :].reshape(L * R, C)
    sums = []
    for values in (field * ext[AP, 0:L, 0:R, :].reshape(L * R, C), field):
        high, low = split(values)
        picked = jnp.dot(high, hot, preferred_element_type=F32) + jnp.dot(
            low, hot, preferred_element_type=F32
        )
        part = jnp.zeros((1, 128), F32)
        for g in range(GROUPS):
            chosen = picked[:, 128 * g : 128 * g + 128] * rows[g][0 : L * R]
            part = part + index[g] * jnp.sum(chosen, axis=0, keepdims=True)
        part = part + pltpu.roll(part, 64, 1)
        sums.append(part + pltpu.roll(part, 32, 1))
    aim = four(tgt[...])
    mode = four(ctl[...].astype(F32))
    tile_out[0:1] = sums[0]
    tile_out[1:2] = sums[1]
    tile_out[2:3] = aim
    tile_out[3:4] = mode
    tile_out[4:8] = jnp.zeros((4, 128), F32)
    tiles[4 + gz] = tile_out[...]

    def tile_copy(dx, dz, z):
        slot = 4 * (1 - dx) + z
        sem = 28 + 7 * (dx + 1) + dz + 3
        return pltpu.make_async_remote_copy(
            src_ref=tile_out,
            dst_ref=tiles.at[slot],
            send_sem=send_sem.at[sem],
            recv_sem=recv_sem.at[sem],
            device_id=(gx + dx, gz + dz),
            device_id_type=MESH,
        )

    ties = []
    for dx in (-1, 0, 1):
        for dz in range(-3, 4):
            if dx == 0 and dz == 0:
                continue
            out = (gz + dz >= 0) & (gz + dz < count_z)
            came = (gz - dz >= 0) & (gz - dz < count_z)
            if dx:
                out = out & has["x", 1 if dx > 0 else 0]
                came = came & has["x", 0 if dx > 0 else 1]
            ties.append((out, came, dx, dz))
    for out, _, dx, dz in ties:

        @pl.when(out)
        def _():
            tile_copy(dx, dz, gz).start()

    index_sum[:, 0:R, :] = scatter(own_hot[...], column_values(column, index)).reshape(X, R, C)
    for s in (0, 1):
        for _, came, copy in early[6 * s : 6 * s + 2]:

            @pl.when(came)
            def _():
                copy.wait_recv()

        cell = lane_groups(pc[1 + s])
        index = lane_groups(pi[1 + s])
        for g in range(GROUPS):
            side_hot[:, 512 * s + 128 * g : 512 * s + 128 * g + 128] = one_hot(
                X * 8, side_rows(cell[g], gz, s)
            ).astype(BF16)
            cols[1 + s, g : g + 1] = cell_parts(cell[g], gz)[2]
            idxs[1 + s, g : g + 1] = index[g]
        part = scatter(
            side_hot[:, 512 * s : 512 * s + 512],
            column_values([cell_parts(v, gz)[2] for v in cell], index),
        ).reshape(X, 8, C)
        if s == 0:
            index_sum[:, R:X, :] = part
        else:
            index_sum[:, R:X, :] += part

    for n, (_, came, copy) in enumerate(early):
        if n % 6 < 2:
            continue

        @pl.when(came)
        def _():
            copy.wait_recv()

    for s, base in ((0, LO), (1, HI)):
        for n, a in enumerate(PACKED):
            for i in range(H):
                ext[a, 0:L, base + i, :] = raw_in[s, 4 * n + i]
    for _, came, copy in late:

        @pl.when(came)
        def _():
            copy.wait_recv()

    for s, base in ((0, LO), (1, HI)):
        for i in range(H):
            ext[ATO, 0:L, base + i, :] = cmp_in[s, i]
        frac[0:L, X - 1 if s == 0 else HI, :] = cmp_in[s, 4]
        for t in (0, 1):
            l0 = LO if t == 0 else HI
            for n, pair in enumerate(PAIRS):
                for i in range(H):
                    for h, a in enumerate(pair):
                        ext[a, l0 : l0 + H, base + i, :] = corner_in[
                            2 * s + t, 4 * n + i, 4 * h : 4 * h + 4, :
                        ]

    for out, came, dx, dz in ties:

        @pl.when(came)
        def _():
            tile_copy(dx, dz, gz - dz).wait_recv()

    for out, _, copy in early + late:

        @pl.when(out)
        def _():
            copy.wait_send()

    for out, _, dx, dz in ties:

        @pl.when(out)
        def _():
            tile_copy(dx, dz, gz).wait_send()

    loads[9].wait()


def shift_rows(value, by):
    return pltpu.roll(value, by % value.shape[0], 0)


def shift_columns(value, by):
    return pltpu.roll(value, by % C, 1)


def solve(
    count_x,
    count_z,
    ext,
    frac,
    local,
    index_sum,
    own_hot,
    side_hot,
    cols,
    idxs,
    edge_x,
    edge_z,
    tiles,
    new_p,
    residual,
    new_s,
    new_h,
    hole,
    coef,
    face,
    source,
    field,
    out_p,
    out_r,
    out_s,
    out_h,
    sems,
):
    gx, gz = lax.axis_index("gx"), lax.axis_index("gz")

    holes = []
    for d in range(3):
        tile = tiles[4 * d] + tiles[4 * d + 1] + tiles[4 * d + 2] + tiles[4 * d + 3]
        sum_p, sum_w = tile[0:1], tile[1:2]
        aim, mode = tiles[4 * d][2:3], tiles[4 * d][3:4]
        holes.append(jnp.where(mode == 0.0, (aim + sum_p) / sum_w, aim))
    hole[...] = holes[1][:, 0:WELLS]

    def spread(n, bottom):
        return column_values(
            [cols[n, g : g + 1] for g in range(GROUPS)],
            [idxs[n, g : g + 1] * bottom for g in range(GROUPS)],
        )

    source[:, 0:R, :] = scatter(own_hot[...], spread(0, holes[1])).reshape(X, R, C)
    source[:, R:X, :] = scatter(
        side_hot[...], jnp.concatenate([spread(1, holes[0]), spread(2, holes[2])], axis=1)
    ).reshape(X, 8, C)

    row = lax.broadcasted_iota(jnp.int32, (X, C), 0)
    column = lax.broadcasted_iota(jnp.int32, (X, C), 1)
    cut_row = (row == LO - 1) | ((row == R - 1) & (gx == count_x - 1))
    row_half = jnp.where(cut_row, 0.0, 0.5)
    column_half = jnp.where(column == C - 1, 0.0, 0.5)
    layer_half = jnp.where(gz == count_z - 1, 0.0, 0.5)
    tail = lax.broadcasted_iota(jnp.int32, (8, C), 0)

    def layer_face(l):
        if l == LO - 1:
            return jnp.zeros((X, C), F32)
        half = layer_half if l == L - 1 else 0.5
        return ext[AT0, l] * half * (ext[ATO, l] + ext[ATO, (l + 1) % X])

    below = layer_face(X - 1)
    for l in range(X):
        total, p, storage = ext[ATO, l], ext[AP, l], ext[AST, l]
        above = layer_face(l)
        next_row = ext[AT1, l] * row_half * (total + shift_rows(total, -1))
        prev_row = shift_rows(next_row, 1)
        next_col = ext[AT2, l] * column_half * (total + shift_columns(total, -1))
        prev_col = shift_columns(next_col, 1)
        src = total * (source[l] - p * index_sum[l])
        diag = storage + above + below + next_row + prev_row + next_col + prev_col
        rhs = storage * p + src
        if l < L:
            source[l] = src
            low, high = edge_x[0, :, l : l + 1, :], edge_x[1, :, l : l + 1, :]
            pick = [
                jnp.where(tail == 3, high[n], jnp.where(tail == 4, low[n], 0.0)) for n in (0, 1)
            ]
            pad = jnp.zeros((R, C), F32)
            diag = diag + jnp.concatenate([pad, pick[0]], axis=0)
            rhs = rhs + jnp.concatenate([pad, pick[1]], axis=0)
        elif l in (LO - 1, LO):
            side = edge_z[1 if l == LO - 1 else 0]
            pad = jnp.zeros((X - R, C), F32)
            diag = diag + jnp.concatenate([side[0], pad], axis=0)
            rhs = rhs + jnp.concatenate([side[1], pad], axis=0)
        inverse = 1.0 / diag
        for n, value in enumerate((rhs, above, below, next_row, prev_row, next_col, prev_col)):
            coef[n, l] = value * inverse
        if l < L or l == X - 1:
            face[0, l] = above
            face[1, l] = next_row
            face[2, l] = next_col
        below = above

    for sweep in range(4):
        layers = [l % X for l in range(-(3 - sweep) - 1, L + 4 - sweep)]
        for l in layers:
            if sweep == 0:
                p, up, down = ext[AP, l], ext[AP, (l + 1) % X], ext[AP, (l - 1) % X]
            else:
                old = (sweep - 1) % 2
                p, up, down = field[old, l], field[old, (l + 1) % X], field[old, (l - 1) % X]
            field[sweep % 2, l] = (
                coef[0, l]
                + coef[1, l] * up
                + coef[2, l] * down
                + coef[3, l] * shift_rows(p, -1)
                + coef[4, l] * shift_rows(p, 1)
                + coef[5, l] * shift_columns(p, -1)
                + coef[6, l] * shift_columns(p, 1)
            )

    writes = []
    final = 1

    def layer_flow(l):
        k, n = l % X, (l + 1) % X
        flow = face[0, k, 0:R, :] * (field[final, k, 0:R, :] - field[final, n, 0:R, :])
        return flow, flow * jnp.where(flow > 0, frac[k, 0:R, :], frac[n, 0:R, :])

    below, gas_below = layer_flow(-1)
    for l in range(L):
        p, part = field[final, l], frac[l]
        above, gas_above = layer_flow(l)
        flow = face[1, l] * (p - shift_rows(p, -1))
        gas = flow * jnp.where(flow > 0, part, shift_rows(part, -1))
        net = (flow - shift_rows(flow, 1))[0:R] + above - below
        out = (gas - shift_rows(gas, 1))[0:R] + gas_above - gas_below
        p, part = p[0:R], part[0:R]
        flow = face[2, l, 0:R, :] * (p - shift_columns(p, -1))
        gas = flow * jnp.where(flow > 0, part, shift_columns(part, -1))
        net = net + flow - shift_columns(flow, 1)
        out = out + gas - shift_columns(gas, 1)
        src = source[l, 0:R, :]
        out_p[l] = p
        out_r[l] = ext[AST, l, 0:R, :] * (ext[AP, l, 0:R, :] - p) + src - net
        gas_source = jnp.maximum(src, 0.0) + jnp.minimum(src, 0.0) * part
        saturation = local[0, l] + local[2, l] * (gas_source - out)
        out_s[l] = saturation
        out_h[l] = jnp.maximum(local[1, l], saturation)
        below, gas_below = above, gas_above
    for n, (src, dst) in enumerate(
        ((out_p, new_p), (out_r, residual), (out_s, new_s), (out_h, new_h))
    ):
        copy = pltpu.make_async_copy(src, dst, sems.at[n])
        copy.start()
        writes.append(copy)
    for copy in writes:
        copy.wait()


def body(
    count_x,
    count_z,
    pressure,
    saturation,
    sat_history,
    storage,
    step_volume,
    transmiss,
    perf_cell,
    perf_index,
    control,
    target,
):
    vmem = pl.BlockSpec(memory_space=pltpu.VMEM)
    hbm = pl.BlockSpec(memory_space=pltpu.HBM)
    dma = pltpu.SemaphoreType.DMA
    block = (L, R, C)
    mid = pl.pallas_call(
        functools.partial(exchange, count_x, count_z),
        out_shape=(
            pltpu.VMEM((6, X, X, C), F32),
            pltpu.VMEM((X, X, C), F32),
            pltpu.VMEM((3, *block), F32),
            pltpu.VMEM((X, X, C), F32),
            pltpu.VMEM((X * R, 512), BF16),
            pltpu.VMEM((X * 8, 1024), BF16),
            pltpu.VMEM((3, 8, 128), jnp.int32),
            pltpu.VMEM((3, 8, 128), F32),
            pltpu.VMEM((2, 2, L, C), F32),
            pltpu.VMEM((2, 2, R, C), F32),
            pltpu.VMEM((12, 8, 128), F32),
        ),
        in_specs=[hbm] * 10,
        out_specs=[vmem] * 11,
        scratch_shapes=[
            pltpu.VMEM((2, RAW, L, C), F32),
            pltpu.VMEM((2, RAW, L, C), F32),
            pltpu.VMEM((2, 7, L, C), F32),
            pltpu.VMEM((2, 5, L, C), F32),
            pltpu.VMEM((4, 12, 8, C), F32),
            pltpu.VMEM((4, 12, 8, C), F32),
            pltpu.VMEM((2, 2, R, C), F32),
            pltpu.VMEM((8, 128), F32),
            pltpu.VMEM((3, NP, WELLS), jnp.int32),
            pltpu.VMEM((3, NP, WELLS), F32),
            pltpu.VMEM((1, WELLS), jnp.int32),
            pltpu.VMEM((1, WELLS), F32),
            dma((10,)),
            dma((49,)),
            dma((49,)),
        ],
        compiler_params=pltpu.CompilerParams(
            collective_id=0, has_side_effects=True, vmem_limit_bytes=VMEM_LIMIT
        ),
        name="exchange",
    )(
        pressure,
        saturation,
        sat_history,
        storage,
        step_volume,
        transmiss,
        perf_cell.T,
        perf_index.T,
        control.reshape(1, WELLS),
        target.reshape(1, WELLS),
    )
    whole = jax.ShapeDtypeStruct(block, F32)
    *fields, hole = pl.pallas_call(
        functools.partial(solve, count_x, count_z),
        out_shape=(whole, whole, whole, whole, jax.ShapeDtypeStruct((1, WELLS), F32)),
        in_specs=[vmem] * 11,
        out_specs=[hbm] * 4 + [vmem],
        scratch_shapes=[
            pltpu.VMEM((7, X, X, C), F32),
            pltpu.VMEM((3, X, X, C), F32),
            pltpu.VMEM((X, X, C), F32),
            pltpu.VMEM((2, X, X, C), F32),
            pltpu.VMEM(block, F32),
            pltpu.VMEM(block, F32),
            pltpu.VMEM(block, F32),
            pltpu.VMEM(block, F32),
            dma((4,)),
        ],
        compiler_params=pltpu.CompilerParams(vmem_limit_bytes=VMEM_LIMIT),
        name="solve",
    )(*mid)
    return (*fields, hole.reshape(WELLS))


def solution(mesh):
    cells = P("gz", "gx", None)
    return jax.shard_map(
        functools.partial(body, mesh.shape["gx"], mesh.shape["gz"]),
        mesh=mesh,
        in_specs=(
            *[cells] * 5,
            P(None, "gz", "gx", None),
            P("gx", None),
            P("gx", None),
            P("gx"),
            P("gx"),
        ),
        out_specs=(*[cells] * 4, P("gx")),
        check_vma=False,
    )
```

```python
import functools

import jax
import jax.numpy as jnp
from jax import lax
from jax.experimental import pallas as pl
from jax.experimental.pallas import tpu as pltpu
from jax.sharding import PartitionSpec as P

L = 16
R = 16
C = 256
WELLS = 32
NP = 16
GROUPS = WELLS * NP // 128
SIDES = range(4)
MESH = pl.DeviceIdType.MESH
F32 = jnp.float32
BF16 = jnp.bfloat16
VMEM_LIMIT = 26 * 2**20


def mobility(sat, history):
    trapped = history / (1.0 + 1.5 * history)
    excess = jnp.maximum(sat - trapped, 0.0)
    free_gas = 0.5 * (excess + jnp.sqrt(excess * excess + excess / 0.375))
    relperm = jnp.where(sat < history, free_gas * free_gas, sat * sat)
    gas = relperm / 0.5
    total = (1.0 - sat) * (1.0 - sat) + gas
    return (total, gas / total)


def split(values):
    high = values.astype(BF16)
    low = (values - high.astype(F32)).astype(BF16)
    return high, low


def four(row):
    return jnp.concatenate([row, row, row, row], axis=1)


def lane_groups(table):
    wide = four(table)
    place = lax.broadcasted_iota(jnp.int32, (1, 128), 1) // WELLS
    rows = []
    for g in range(GROUPS):
        row = wide[4 * g : 4 * g + 1]
        for k in range(1, 4):
            row = jnp.where(place == k, wide[4 * g + k : 4 * g + k + 1], row)
        rows.append(row)
    return rows


def cell_parts(cell, gz):
    layer = lax.shift_right_logical(cell, 12) - gz * L
    return layer, lax.shift_right_logical(cell, 8) & (R - 1), cell & (C - 1)


def one_hot(size, target):
    return jnp.where(lax.broadcasted_iota(jnp.int32, (size, 128), 0) == target, 1.0, 0.0)


def own_rows(cell, gz):
    layer, row, _ = cell_parts(cell, gz)
    index = jnp.where(layer == -1, L + 1, layer)
    return jnp.where((layer >= -1) & (layer <= L), index * R + row, -1)


def side_rows(cell, gz, side):
    layer, row, _ = cell_parts(cell, gz)
    return jnp.where((layer >= 0) & (layer < L) & (row == (0 if side else R - 1)), layer, -1)


def column_values(columns, values):
    place = lax.broadcasted_iota(jnp.int32, (C, 128), 0)
    return jnp.concatenate(
        [jnp.where(place == c, v, 0.0) for c, v in zip(columns, values)], axis=1
    )


def shift_rows(value, by):
    return pltpu.roll(value, by % value.shape[0], 0)


def shift_columns(value, by):
    return pltpu.roll(value, by % C, 1)


def near_end(side):
    return 15 * (side % 2)


def plane(ref, side, k):
    return ref[0:L, k, :] if side < 2 else ref[k, 0:R, :]


def add_to_plane(ref, side, k, value):
    if side < 2:
        ref[0:L, k, :] += value
    else:
        ref[k, 0:R, :] += value


def ends(side):
    for e in (0, 1):
        yield e, 15 * e, 2 * side + e if side < 2 else 2 * e + side - 2


def planes(ref, side, n):
    return ref[side, 16 * n : 16 * n + 16]


def inner_sum(start, p, up, down, above, below, next_row, next_col):
    value = start + next_row * shift_rows(p, -1) + shift_rows(next_row * p, 1)
    value = value + next_col * shift_columns(p, -1) + shift_columns(next_col * p, 1)
    if up is not None:
        value = value + above * up
    if down is not None:
        value = value + below * down
    return value


def sweep_layer(ref, rhs, face, l):
    return inner_sum(
        rhs[l],
        ref[l],
        ref[l + 1] if l < L - 1 else None,
        ref[l - 1] if l else None,
        face[0, l],
        face[0, l - 1] if l else None,
        face[1, l],
        face[2, l],
    )


def exchange(
    count_x,
    count_z,
    p_in,
    sat_in,
    hist_in,
    sto_in,
    vol_in,
    tr_in,
    pc_in,
    pi_in,
    ctl_in,
    tgt_in,
    storage,
    local,
    frac,
    face,
    inverse,
    rhs,
    source,
    second,
    third,
    border,
    weight,
    over_ring,
    end_face,
    over_corner,
    bulk_in,
    mid_in,
    last_in,
    last_corner_in,
    hole,
    p0,
    total,
    trans,
    num,
    diag,
    first,
    ring,
    index_sum,
    side_index,
    own_source,
    side_source,
    own_hot,
    side_hot,
    column_hot,
    spread,
    near_out,
    near_in,
    corner_out,
    corner_in,
    bulk_out,
    mid_out,
    last_out,
    last_corner_out,
    perf_out,
    perf_in,
    tile_out,
    tiles,
    pc,
    pi,
    ctl,
    tgt,
    send_sem,
    recv_sem,
):
    gx, gz = lax.axis_index("gx"), lax.axis_index("gz")
    has = (gx > 0, gx < count_x - 1, gz > 0, gz < count_z - 1)

    barrier = pltpu.get_barrier_semaphore()

    def signal_column(x):
        def one(z, carry):
            pl.semaphore_signal(barrier, inc=1, device_id=(x, z), device_id_type=MESH)
            return carry

        return one

    def others(z, carry):
        @pl.when(z != gz)
        def _():
            pl.semaphore_signal(barrier, inc=1, device_id=(gx, z), device_id_type=MESH)

        return carry

    for s in (0, 1):

        @pl.when(has[s])
        def _():
            lax.fori_loop(0, count_z, signal_column(gx + 2 * s - 1), 0)

    lax.fori_loop(0, count_z, others, 0)

    loads = [
        pltpu.make_async_copy(pc_in, pc, send_sem.at[0]),
        pltpu.make_async_copy(pi_in, pi, send_sem.at[1]),
        pltpu.make_async_copy(sat_in, local.at[0], send_sem.at[2]),
        pltpu.make_async_copy(hist_in, local.at[1], send_sem.at[3]),
        pltpu.make_async_copy(p_in, p0, send_sem.at[4]),
        pltpu.make_async_copy(ctl_in, ctl, send_sem.at[5]),
        pltpu.make_async_copy(tgt_in, tgt, send_sem.at[6]),
        pltpu.make_async_copy(tr_in, trans, send_sem.at[7]),
        pltpu.make_async_copy(sto_in, storage, send_sem.at[8]),
        pltpu.make_async_copy(vol_in, local.at[2], send_sem.at[9]),
    ]
    for copy in loads:
        copy.start()

    for side in SIDES:

        @pl.when(jnp.logical_not(has[side]))
        def _():
            near_in[side] = jnp.zeros((88, C), F32)
            near_in[side, 48:64] = jnp.ones((16, C), F32)
            bulk_in[side] = jnp.zeros((64, C), F32)
            mid_in[side] = jnp.zeros((24, C), F32)
            last_in[side] = jnp.zeros((48, C), F32)
            if side < 2:
                perf_in[side] = jnp.where(
                    lax.broadcasted_iota(jnp.int32, (NP, 128), 1) < WELLS, 1e9, 0.0
                )
                tiles[8 * side : 8 * side + 4] = jnp.ones((4, 1, 128), F32)

    for c in range(4):

        @pl.when(jnp.logical_not(has[c // 2] & has[2 + c % 2]))
        def _():
            corner_in[c] = jnp.zeros((8, C), F32)
            corner_in[c, 4:5] = jnp.ones((1, C), F32)
            last_corner_in[c] = jnp.zeros((4, C), F32)

    for n in (0, 1):
        loads[n].wait()
    cell = lane_groups(pc[...])
    own_index = lane_groups(pi[...])
    own_column = [cell_parts(v, gz)[2] for v in cell]
    own_row = [own_rows(v, gz) for v in cell]
    for g in range(GROUPS):
        part = slice(128 * g, 128 * g + 128)
        own_hot[:, part] = one_hot((L + 2) * R, own_row[g]).astype(BF16)
        column_hot[:, part] = one_hot(C, own_column[g]).astype(BF16)
    table = jnp.concatenate([pc[...].astype(F32), pi[...]], axis=1)
    perf_out[...] = jnp.concatenate([table, table], axis=1)

    for n in (2, 3):
        loads[n].wait()
    for l in range(L):
        total[l], frac[l] = mobility(local[0, l], local[1, l])
    for n in (4, 7, 8):
        loads[n].wait()

    row = lax.broadcasted_iota(jnp.int32, (R, C), 0)
    column = lax.broadcasted_iota(jnp.int32, (R, C), 1)
    row_half = jnp.where(row == R - 1, 0.0, 0.5)
    column_half = jnp.where(column == C - 1, 0.0, 0.5)
    below = None
    for l in range(L):
        here = total[l]
        next_row = trans[1, l] * row_half * (here + shift_rows(here, -1))
        next_col = trans[2, l] * column_half * (here + shift_columns(here, -1))
        above = trans[0, l] * 0.5 * (here + total[l + 1]) if l < L - 1 else None
        num[l] = inner_sum(
            storage[l] * p0[l],
            p0[l],
            p0[l + 1] if l < L - 1 else None,
            p0[l - 1] if l else None,
            above,
            below,
            next_row,
            next_col,
        )
        bottom = storage[l] + next_row + shift_rows(next_row, 1)
        bottom = bottom + next_col + shift_columns(next_col, 1)
        if l:
            bottom = bottom + below
        if l < L - 1:
            bottom = bottom + above
        diag[l] = bottom
        face[0, l] = above if l < L - 1 else jnp.zeros((R, C), F32)
        face[1, l] = next_row
        face[2, l] = next_col
        below = above

    for side in SIDES:
        k = 15 - near_end(side)
        normal, along = (1, 0) if side < 2 else (0, 1)
        for n, ref in enumerate((p0, total, num, diag, trans.at[normal])):
            near_out[side, 16 * n : 16 * n + 16] = plane(ref, side, k)
        if side < 2:
            near_out[side, 80:81] = trans[along, L - 1, k : k + 1, :]
        else:
            near_out[side, 80:81] = trans[along, k, R - 1 : R, :]
        behind = min(k, 14)
        for n, (ref, at) in enumerate(
            ((face.at[along], k), (face.at[normal], behind), (face.at[2], k), (frac, k))
        ):
            bulk_out[side, 16 * n : 16 * n + 16] = plane(ref, side, at)
    for c in range(4):
        k, m = 15 - 15 * (c // 2), 15 - 15 * (c % 2)
        for n, ref in enumerate((p0, total, trans.at[0], trans.at[1], diag)):
            corner_out[c, n : n + 1] = ref[m, k : k + 1, :]

    for n in (5, 6, 9):
        loads[n].wait()
    field = total[...].reshape(L * R, C)
    parts = split(field * p0[...].reshape(L * R, C)) + split(field)
    picked = jnp.dot(
        jnp.concatenate(parts, axis=0), column_hot[...], preferred_element_type=F32
    )
    place = lax.broadcasted_iota(jnp.int32, (L * R, 128), 0)
    sums = []
    for n in (0, 1):
        part = jnp.zeros((1, 128), F32)
        for g in range(GROUPS):
            pair = picked[2 * n * L * R : 2 * (n + 1) * L * R, 128 * g : 128 * g + 128]
            chosen = jnp.where(place == own_row[g], pair[0 : L * R] + pair[L * R :], 0.0)
            part = part + own_index[g] * jnp.sum(chosen, axis=0, keepdims=True)
        part = part + pltpu.roll(part, 64, 1)
        sums.append(part + pltpu.roll(part, 32, 1))
    quarter = lax.broadcasted_iota(jnp.int32, (1, 128), 1) // WELLS
    packed = jnp.where(quarter == 0, sums[0], sums[1])
    packed = jnp.where(quarter == 2, four(tgt[...]), packed)
    packed = jnp.where(quarter == 3, four(ctl[...].astype(F32)), packed)
    tile_out[...] = packed
    tiles[4 + gz] = packed

    pl.semaphore_wait(
        barrier, count_z * (1 + has[0].astype(jnp.int32) + has[1].astype(jnp.int32)) - 1
    )

    def target(side):
        step = 1 - 2 * (side % 2)
        return (gx + step, gz) if side < 2 else (gx, gz + step)

    def remote(src, dst, send, recv, device):
        return pltpu.make_async_remote_copy(
            src_ref=src,
            dst_ref=dst,
            send_sem=send_sem.at[send],
            recv_sem=recv_sem.at[recv],
            device_id=device,
            device_id_type=MESH,
        )

    near, perf, bulk, mid, last = [], [], [], [], []
    for c in range(4):
        s, t = c // 2, 2 + c % 2
        ok = (has[s ^ 1] & has[t ^ 1], has[s] & has[t])
        to = (target(s)[0], target(t)[1])
        near.append((*ok, remote(corner_out.at[c], corner_in.at[c], 4 + c, 4 + c, to)))
        last.append((*ok, remote(last_corner_out.at[c], last_corner_in.at[c], 4 + c, 18 + c, to)))
    for side in SIDES:
        ok, to = (has[side ^ 1], has[side]), target(side)
        near.append((*ok, remote(near_out.at[side], near_in.at[side], side, side, to)))
        bulk.append((*ok, remote(bulk_out.at[side], bulk_in.at[side], 22 + side, 10 + side, to)))
        mid.append((*ok, remote(mid_out.at[side], mid_in.at[side], side, 34 + side, to)))
        last.append((*ok, remote(last_out.at[side], last_in.at[side], 22 + side, 14 + side, to)))
    for side in (0, 1):
        ok, to = (has[side ^ 1], has[side]), target(side)
        perf.append((*ok, remote(perf_out, perf_in.at[side], 8 + side, 8 + side, to)))

    def start(copies):
        for out, _, copy in copies:

            @pl.when(out)
            def _():
                copy.start()

    def arrive(copies):
        for _, came, copy in copies:

            @pl.when(came)
            def _():
                copy.wait_recv()

    def sent(copies):
        for out, _, copy in copies:

            @pl.when(out)
            def _():
                copy.wait_send()

    def tile_copy(dx, z_from, z_to):
        return pltpu.make_async_remote_copy(
            src_ref=tile_out,
            dst_ref=tiles.at[4 * (1 - dx) + z_from],
            send_sem=send_sem.at[10 + 4 * (1 - dx) + z_to],
            recv_sem=recv_sem.at[22 + 4 * (1 - dx) + z_from],
            device_id=(gx + dx, z_to),
            device_id_type=MESH,
        )

    start(perf)
    ties = []
    for dx in (1, -1, 0):
        for z in range(4):
            if dx:
                ok = (has[1 if dx > 0 else 0], has[0 if dx > 0 else 1])
            else:
                ok = (gz != z, gz != z)
            ties.append((*ok, dx, z))
    for out, _, dx, z in ties:

        @pl.when(out)
        def _():
            tile_copy(dx, gz, z).start()

    start(near)

    start(bulk)

    def place_index(d, columns, indices):
        high, low = split(column_values(columns, indices).T)
        spread[0, 512 * d : 512 * d + 512, :] = high
        spread[1, 512 * d : 512 * d + 512, :] = low

    def product(rows, n, d):
        return jnp.dot(
            rows, spread[n, 512 * d : 512 * d + 512, :], preferred_element_type=F32
        )

    place_index(2, own_column, own_index)
    index_sum[...] = (product(own_hot[...], 0, 2) + product(own_hot[...], 1, 2)).reshape(
        L + 2, R, C
    )
    arrive(perf)
    for side in (0, 1):
        table = perf_in[side]
        cell = lane_groups(table[:, 0:WELLS].astype(jnp.int32))
        for g in range(GROUPS):
            side_hot[side, :, 128 * g : 128 * g + 128] = one_hot(
                L, side_rows(cell[g], gz, side)
            ).astype(BF16)
        place_index(
            side,
            [cell_parts(v, gz)[2] for v in cell],
            lane_groups(table[:, WELLS : 2 * WELLS]),
        )
        side_index[side] = product(side_hot[side], 0, side) + product(side_hot[side], 1, side)

    for _, came, dx, z in ties:

        @pl.when(came)
        def _():
            tile_copy(dx, z, gz).wait_recv()

    def scaled(rows, group, d):
        parts = [tiles[4 * group + z] for z in range(4)]
        tile = parts[0] + parts[1] + parts[2] + parts[3]
        sum_p, sum_w = tile[:, 0:WELLS], tile[:, WELLS : 2 * WELLS]
        aim, mode = parts[0][:, 2 * WELLS : 3 * WELLS], parts[0][:, 3 * WELLS : 4 * WELLS]
        bottom = jnp.where(mode == 0.0, (aim + sum_p) / sum_w, aim)
        high, low = split(jnp.concatenate([four(bottom)] * GROUPS, axis=1))
        high, low = rows * high, rows * low
        return bottom, product(high, 0, d) + product(high, 1, d) + product(low, 0, d)

    bottom, values = scaled(own_hot[...], 1, 2)
    hole[...] = bottom
    own_source[...] = values.reshape(L + 2, R, C)
    for side in (0, 1):
        side_source[side] = scaled(side_hot[side], 2 * side, side)[1]

    arrive(near)

    for side in SIDES:
        k = near_end(side)
        p, here = planes(near_in, side, 0), planes(near_in, side, 1)
        across = planes(near_in, side, 4)
        if side % 2:
            across = plane(trans.at[1 if side < 2 else 0], side, k)
        rate = across * jnp.where(has[side], 0.5, 0.0) * (plane(total, side, k) + here)
        border[side] = rate
        add_to_plane(diag, side, k, rate)
        if side < 2:
            well, index = side_source[side], side_index[side]
        else:
            n = L + 1 if side == 2 else L
            well, index = own_source[n], index_sum[n]
        ring[side] = planes(near_in, side, 2) + rate * plane(p0, side, k) + here * (well - p * index)
        over_ring[side] = planes(near_in, side, 3) + rate
        for e, at, c in ends(side):
            cell = corner_in[c]
            if e:
                rate = near_in[side, 80:81]
            else:
                rate = cell[2:3] if side < 2 else cell[3:4]
            rate = rate * jnp.where(has[c // 2] & has[2 + c % 2], 0.5, 0.0)
            rate = rate * (near_in[side, 16 + at : 17 + at] + cell[1:2])
            end_face[2 * side + e] = rate
            ring[side, at : at + 1] += rate * cell[0:1]
            over_ring[side, at : at + 1] += rate
        over_ring[side] = 1.0 / over_ring[side]
        ring[side] *= over_ring[side]
    for c in range(4):
        s, t = c // 2, c % 2
        over_corner[c] = 1.0 / (
            corner_in[c, 4:5] + end_face[2 * s + t] + end_face[2 * (2 + t) + s]
        )

    for l in range(L):
        src = total[l] * (own_source[l] - p0[l] * index_sum[l])
        over = 1.0 / diag[l]
        inverse[l] = over
        source[l] = src
        rhs[l] = storage[l] * p0[l] + src
        first[l] = (num[l] + src) * over
    for side in SIDES:
        k = near_end(side)
        part = border[side] * plane(inverse, side, k)
        weight[side] = part
        add_to_plane(first, side, k, part * planes(near_in, side, 0))

    sent(near)
    for side in SIDES:
        k = 15 - near_end(side)
        behind = 14 if k else 1
        mid_out[side, 0:16] = plane(rhs, side, k)
        for e in (0, 1):
            other = 2 + e if side < 2 else e
            mid_out[side, 16 + e : 17 + e] = weight[other, behind : behind + 1]
    start(mid)

    for l in range(L):
        second[l] = sweep_layer(first, rhs, face, l) * inverse[l]
    for side in SIDES:
        add_to_plane(second, side, near_end(side), weight[side] * ring[side])

    for l in range(L):
        value = sweep_layer(second, rhs, face, l)
        num[l] = value
        third[l] = value * inverse[l]

    sent(bulk)
    for side in SIDES:
        k = 15 - near_end(side)
        behind = 14 if k else 1
        for n, (ref, at) in enumerate(((second, k), (num, k), (third, behind))):
            last_out[side, 16 * n : 16 * n + 16] = plane(ref, side, at)
    for c in range(4):
        k, m = 15 - 15 * (c // 2), 15 - 15 * (c % 2)
        k2, m2 = 14 if k else 1, 14 if m else 1
        last_corner_out[c, 0:1] = second[m, k : k + 1, :]
        last_corner_out[c, 1:2] = num[m, k : k + 1, :]
        last_corner_out[c, 2:3] = second[m, k2 : k2 + 1, :]
        last_corner_out[c, 3:4] = second[m2, k : k + 1, :]
    start(last)

    sent(perf)
    for out, _, dx, z in ties:

        @pl.when(out)
        def _():
            tile_copy(dx, gz, z).wait_send()

    arrive(bulk)

    arrive(mid)
    sent(mid)

    arrive(last)
    sent(last)


def solve(
    storage,
    local,
    frac,
    face,
    inverse,
    rhs,
    source,
    second,
    third,
    border,
    weight,
    over_ring,
    end_face,
    over_corner,
    bulk_in,
    mid_in,
    last_in,
    last_corner_in,
    hole,
    new_p,
    residual,
    new_s,
    new_h,
    new_hole,
    fourth,
    flows,
    out_r,
    out_s,
    out_h,
    sems,
):
    new_hole[...] = hole[...]
    spot = lax.broadcasted_iota(jnp.int32, (16, C), 0)
    corners = []
    for c in range(4):
        s, t = c // 2, c % 2
        value = last_corner_in[c, 1:2]
        value = value + end_face[2 * s + t] * last_in[s, 15 * t : 15 * t + 1]
        value = value + end_face[2 * (2 + t) + s] * last_in[2 + t, 15 * s : 15 * s + 1]
        corners.append(value * over_corner[c])
    rings, parts = [], []
    for side in SIDES:
        k = near_end(side)
        rate = border[side]
        value = planes(last_in, side, 1) + rate * plane(second, side, k)
        behind = planes(last_in, side, 2)
        add = jnp.zeros((16, C), F32)
        for e, at, c in ends(side):
            cell = last_corner_in[c]
            value = value + jnp.where(spot == at, end_face[2 * side + e] * cell[0:1], 0.0)
            far = cell[2:3] if side < 2 else cell[3:4]
            behind = behind + jnp.where(spot == at, mid_in[side, 16 + e : 17 + e] * far, 0.0)
            add = add + jnp.where(spot == at, end_face[2 * side + e] * corners[c], 0.0)
        value = value * over_ring[side]
        rings.append(value)
        along, across, col = (planes(bulk_in, side, n) for n in range(3))
        part = inner_sum(
            planes(mid_in, side, 0) + add, value, behind, None, across, None, along, col
        )
        parts.append(part)
    for side in SIDES:
        add_to_plane(third, side, near_end(side), weight[side] * planes(last_in, side, 0))

    for l in range(L):
        fourth[l] = sweep_layer(third, rhs, face, l) * inverse[l]
    for side in SIDES:
        add_to_plane(fourth, side, near_end(side), weight[side] * rings[side])
    writes = [pltpu.make_async_copy(fourth, new_p, sems.at[0, 3])]
    writes[0].start()
    for side in SIDES:
        k = near_end(side)
        outer = (parts[side] + border[side] * plane(third, side, k)) * over_ring[side]
        flow = border[side] * (plane(fourth, side, k) - outer)
        flows[side, 0] = flow
        flows[side, 1] = flow * jnp.where(flow > 0, plane(frac, side, k), planes(bulk_in, side, 3))

    below = gas_below = None
    for l in range(L):
        p, part = fourth[l], frac[l]
        flow = face[1, l] * (p - shift_rows(p, -1))
        gas = flow * jnp.where(flow > 0, part, shift_rows(part, -1))
        net, out = flow - shift_rows(flow, 1), gas - shift_rows(gas, 1)
        flow = face[2, l] * (p - shift_columns(p, -1))
        gas = flow * jnp.where(flow > 0, part, shift_columns(part, -1))
        net = net + flow - shift_columns(flow, 1)
        out = out + gas - shift_columns(gas, 1)
        for side in (0, 1):
            edge = spot == near_end(side)
            net = net + jnp.where(edge, flows[side, 0, l : l + 1], 0.0)
            out = out + jnp.where(edge, flows[side, 1, l : l + 1], 0.0)
        if l:
            net, out = net - below, out - gas_below
        else:
            net, out = net + flows[2, 0], out + flows[2, 1]
        if l < L - 1:
            below = face[0, l] * (p - fourth[l + 1])
            gas_below = below * jnp.where(below > 0, part, frac[l + 1])
        else:
            below, gas_below = flows[3, 0], flows[3, 1]
        net, out = net + below, out + gas_below
        src = source[l]
        out_r[l] = rhs[l] - storage[l] * p - net
        gas_source = jnp.maximum(src, 0.0) + jnp.minimum(src, 0.0) * part
        saturation = local[0, l] + local[2, l] * (gas_source - out)
        out_s[l] = saturation
        out_h[l] = jnp.maximum(local[1, l], saturation)
        if l % 8 == 7:
            part = pl.ds(l - 7, 8)
            for n, (src, dst) in enumerate(
                ((out_r, residual), (out_s, new_s), (out_h, new_h))
            ):
                copy = pltpu.make_async_copy(src.at[part], dst.at[part], sems.at[l // 8, n])
                copy.start()
                writes.append(copy)
    for copy in writes:
        copy.wait()


def body(
    count_x,
    count_z,
    pressure,
    saturation,
    sat_history,
    storage,
    step_volume,
    transmiss,
    perf_cell,
    perf_index,
    control,
    target,
):
    vmem = pl.BlockSpec(memory_space=pltpu.VMEM)
    hbm = pl.BlockSpec(memory_space=pltpu.HBM)
    dma = pltpu.SemaphoreType.DMA
    block = (L, R, C)
    side = (4, 16, C)
    mid = pl.pallas_call(
        functools.partial(exchange, count_x, count_z),
        out_shape=[
            pltpu.VMEM(shape, F32)
            for shape in (
                block,
                (3, *block),
                block,
                (3, *block),
                *[block] * 5,
                *[side] * 3,
                (8, 1, C),
                (4, 1, C),
                (4, 64, C),
                (4, 24, C),
                (4, 48, C),
                (4, 4, C),
                (1, WELLS),
            )
        ],
        in_specs=[hbm] * 10,
        out_specs=[vmem] * 19,
        scratch_shapes=[
            pltpu.VMEM(block, F32),
            pltpu.VMEM(block, F32),
            pltpu.VMEM((3, *block), F32),
            *[pltpu.VMEM(block, F32)] * 3,
            pltpu.VMEM(side, F32),
            pltpu.VMEM((L + 2, R, C), F32),
            pltpu.VMEM((2, L, C), F32),
            pltpu.VMEM((L + 2, R, C), F32),
            pltpu.VMEM((2, L, C), F32),
            pltpu.VMEM(((L + 2) * R, 512), BF16),
            pltpu.VMEM((2, L, 512), BF16),
            pltpu.VMEM((C, 512), BF16),
            pltpu.VMEM((2, 1536, C), BF16),
            *[pltpu.VMEM((4, 88, C), F32)] * 2,
            *[pltpu.VMEM((4, 8, C), F32)] * 2,
            pltpu.VMEM((4, 64, C), F32),
            pltpu.VMEM((4, 24, C), F32),
            pltpu.VMEM((4, 48, C), F32),
            pltpu.VMEM((4, 4, C), F32),
            pltpu.VMEM((NP, 128), F32),
            pltpu.VMEM((2, NP, 128), F32),
            pltpu.VMEM((1, 128), F32),
            pltpu.VMEM((12, 1, 128), F32),
            pltpu.VMEM((NP, WELLS), jnp.int32),
            pltpu.VMEM((NP, WELLS), F32),
            pltpu.VMEM((1, WELLS), jnp.int32),
            pltpu.VMEM((1, WELLS), F32),
            dma((26,)),
            dma((38,)),
        ],
        compiler_params=pltpu.CompilerParams(
            collective_id=0, has_side_effects=True, vmem_limit_bytes=VMEM_LIMIT
        ),
        name="exchange",
    )(
        *[
            pltpu.with_memory_space_constraint(values, pltpu.HBM)
            for values in (
                pressure,
                saturation,
                sat_history,
                storage,
                step_volume,
                transmiss,
                perf_cell.T,
                perf_index.T,
                control.reshape(1, WELLS),
                target.reshape(1, WELLS),
            )
        ]
    )
    *fields, hole = pl.pallas_call(
        solve,
        out_shape=[jax.ShapeDtypeStruct(block, F32)] * 4
        + [jax.ShapeDtypeStruct((1, WELLS), F32)],
        in_specs=[vmem] * 19,
        out_specs=[hbm] * 4 + [vmem],
        scratch_shapes=[
            pltpu.VMEM(block, F32),
            pltpu.VMEM((4, 2, 16, C), F32),
            *[pltpu.VMEM(block, F32)] * 3,
            dma((2, 4)),
        ],
        compiler_params=pltpu.CompilerParams(vmem_limit_bytes=VMEM_LIMIT),
        name="solve",
    )(*mid)
    return (*fields, hole.reshape(WELLS))


def solution(mesh):
    cells = P("gz", "gx", None)
    return jax.shard_map(
        functools.partial(body, mesh.shape["gx"], mesh.shape["gz"]),
        mesh=mesh,
        in_specs=(
            *[cells] * 5,
            P(None, "gz", "gx", None),
            P("gx", None),
            P("gx", None),
            P("gx"),
            P("gx"),
        ),
        out_specs=(*[cells] * 4, P("gx")),
        check_vma=False,
    )
```

```python
import functools

import jax
import jax.numpy as jnp
from jax import lax
from jax.experimental import pallas as pl
from jax.experimental.pallas import tpu as pltpu
from jax.sharding import PartitionSpec as P

L = 16
R = 16
C = 256
WELLS = 32
NP = 16
GROUPS = WELLS * NP // 128
SIDES = range(4)
MESH = pl.DeviceIdType.MESH
F32 = jnp.float32
BF16 = jnp.bfloat16
VMEM_LIMIT = 26 * 2**20


def mobility(sat, history):
    trapped = history / (1.0 + 1.5 * history)
    excess = jnp.maximum(sat - trapped, 0.0)
    free_gas = 0.5 * (excess + jnp.sqrt(excess * excess + excess / 0.375))
    relperm = jnp.where(sat < history, free_gas * free_gas, sat * sat)
    gas = relperm / 0.5
    total = (1.0 - sat) * (1.0 - sat) + gas
    return (total, gas / total)


def split(values):
    high = values.astype(BF16)
    low = (values - high.astype(F32)).astype(BF16)
    return high, low


def four(row):
    return jnp.concatenate([row, row, row, row], axis=1)


def lane_groups(table):
    wide = four(table)
    place = lax.broadcasted_iota(jnp.int32, (1, 128), 1) // WELLS
    rows = []
    for g in range(GROUPS):
        row = wide[4 * g : 4 * g + 1]
        for k in range(1, 4):
            row = jnp.where(place == k, wide[4 * g + k : 4 * g + k + 1], row)
        rows.append(row)
    return rows


def cell_parts(cell, gz):
    layer = lax.shift_right_logical(cell, 12) - gz * L
    return layer, lax.shift_right_logical(cell, 8) & (R - 1), cell & (C - 1)


def one_hot(size, target):
    return jnp.where(lax.broadcasted_iota(jnp.int32, (size, 128), 0) == target, 1.0, 0.0)


def own_rows(cell, gz):
    layer, row, _ = cell_parts(cell, gz)
    index = jnp.where(layer == -1, L + 1, layer)
    return jnp.where((layer >= -1) & (layer <= L), index * R + row, -1)


def side_rows(cell, gz, side):
    layer, row, _ = cell_parts(cell, gz)
    return jnp.where((layer >= 0) & (layer < L) & (row == (0 if side else R - 1)), layer, -1)


def shift_rows(value, by):
    return pltpu.roll(value, by % value.shape[0], 0)


def shift_columns(value, by):
    return pltpu.roll(value, by % C, 1)


def near_end(side):
    return 15 * (side % 2)


def plane(ref, side, k):
    return ref[0:L, k, :] if side < 2 else ref[k, 0:R, :]


def add_to_plane(ref, side, k, value):
    if side < 2:
        ref[0:L, k, :] += value
    else:
        ref[k, 0:R, :] += value


def set_plane(ref, side, k, value):
    if side < 2:
        ref[0:L, k, :] = value
    else:
        ref[k, 0:R, :] = value


def ends(side):
    for e in (0, 1):
        yield e, 15 * e, 2 * side + e if side < 2 else 2 * e + side - 2


def planes(ref, side, n):
    return ref[side, 16 * n : 16 * n + 16]


def inner_sum(start, p, up, down, above, below, next_row, next_col):
    value = start + next_row * shift_rows(p, -1) + shift_rows(next_row * p, 1)
    value = value + next_col * shift_columns(p, -1) + shift_columns(next_col * p, 1)
    if up is not None:
        value = value + above * up
    if down is not None:
        value = value + below * down
    return value


def sweep_layer(ref, rhs, face, l):
    return inner_sum(
        rhs[l],
        ref[l],
        ref[l + 1] if l < L - 1 else None,
        ref[l - 1] if l else None,
        face[0, l],
        face[0, l - 1] if l else None,
        face[1, l],
        face[2, l],
    )


def exchange(
    count_x,
    count_z,
    p_in,
    sat_in,
    hist_in,
    sto_in,
    vol_in,
    tr_in,
    pc_in,
    pi_in,
    ctl_in,
    tgt_in,
    storage,
    local,
    frac,
    frac_next,
    face,
    inverse,
    rhs,
    source,
    second,
    third,
    fourth,
    border,
    weight,
    over_ring,
    end_face,
    over_corner,
    bulk_in,
    bulk_out,
    last_in,
    last_corner_in,
    hole,
    p0,
    total,
    trans,
    num,
    diag,
    first,
    ring,
    index_sum,
    side_index,
    own_source,
    side_source,
    own_hot,
    column_hot,
    columns_own,
    side_columns,
    near_out,
    near_in,
    corner_out,
    corner_in,
    last_out,
    last_corner_out,
    perf_out,
    perf_in,
    tile_out,
    tiles,
    pc,
    pi,
    ctl,
    tgt,
    send_sem,
    recv_sem,
):
    gx, gz = lax.axis_index("gx"), lax.axis_index("gz")
    has = (gx > 0, gx < count_x - 1, gz > 0, gz < count_z - 1)

    barrier = pltpu.get_barrier_semaphore()

    def signal_column(x):
        def one(z, carry):
            pl.semaphore_signal(barrier, inc=1, device_id=(x, z), device_id_type=MESH)
            return carry

        return one

    def others(z, carry):
        @pl.when(z != gz)
        def _():
            pl.semaphore_signal(barrier, inc=1, device_id=(gx, z), device_id_type=MESH)

        return carry

    for s in (0, 1):

        @pl.when(has[s])
        def _():
            lax.fori_loop(0, count_z, signal_column(gx + 2 * s - 1), 0)

    lax.fori_loop(0, count_z, others, 0)

    loads = [
        pltpu.make_async_copy(pc_in, pc, send_sem.at[0]),
        pltpu.make_async_copy(pi_in, pi, send_sem.at[1]),
        pltpu.make_async_copy(sat_in, local.at[0], send_sem.at[2]),
        pltpu.make_async_copy(hist_in, local.at[1], send_sem.at[3]),
        pltpu.make_async_copy(p_in, p0, send_sem.at[4]),
        pltpu.make_async_copy(ctl_in, ctl, send_sem.at[5]),
        pltpu.make_async_copy(tgt_in, tgt, send_sem.at[6]),
        pltpu.make_async_copy(tr_in, trans, send_sem.at[7]),
        pltpu.make_async_copy(sto_in, storage, send_sem.at[8]),
        pltpu.make_async_copy(vol_in, local.at[2], send_sem.at[9]),
    ]
    for copy in loads:
        copy.start()

    for side in SIDES:

        @pl.when(jnp.logical_not(has[side]))
        def _():
            near_in[side] = jnp.zeros((88, C), F32)
            near_in[side, 64:80] = jnp.ones((16, C), F32)
            bulk_in[side] = jnp.zeros((48, C), F32)
            last_in[side] = jnp.zeros((56, C), F32)
            if side < 2:
                perf_in[side] = jnp.where(
                    lax.broadcasted_iota(jnp.int32, (16, 128), 0) < GROUPS, 1e9, 0.0
                )
                tiles[8 * side : 8 * side + 4] = jnp.ones((4, 1, 128), F32)

    for c in range(4):

        @pl.when(jnp.logical_not(has[c // 2] & has[2 + c % 2]))
        def _():
            corner_in[c] = jnp.zeros((5, C), F32)
            corner_in[c, 4:5] = jnp.ones((1, C), F32)
            last_corner_in[c] = jnp.zeros((4, C), F32)

    for n in (0, 1):
        loads[n].wait()
    cell = lane_groups(pc[...])
    own_index = lane_groups(pi[...])
    own_column = [cell_parts(v, gz)[2] for v in cell]
    own_row = [own_rows(v, gz) for v in cell]
    for g in range(GROUPS):
        part = slice(128 * g, 128 * g + 128)
        own_hot[:, part] = one_hot((L + 2) * R, own_row[g]).astype(BF16)
        column_hot[:, part] = one_hot(C, own_column[g]).astype(BF16)
    for side in (0, 1):
        for g in range(GROUPS):
            perf_out[side, g : g + 1] = cell[g].astype(F32)
            perf_out[side, GROUPS + g : GROUPS + g + 1] = own_index[g]

    for n in (2, 3):
        loads[n].wait()
    for l in range(L):
        total[l], frac[l] = mobility(local[0, l], local[1, l])
    for n in (4, 7, 8):
        loads[n].wait()

    row = lax.broadcasted_iota(jnp.int32, (R, C), 0)
    column = lax.broadcasted_iota(jnp.int32, (R, C), 1)
    row_half = jnp.where(row == R - 1, 0.0, 0.5)
    column_half = jnp.where(column == C - 1, 0.0, 0.5)
    below = None
    for l in range(L):
        here = total[l]
        next_row = trans[1, l] * row_half * (here + shift_rows(here, -1))
        next_col = trans[2, l] * column_half * (here + shift_columns(here, -1))
        above = trans[0, l] * 0.5 * (here + total[l + 1]) if l < L - 1 else None
        num[l] = inner_sum(
            storage[l] * p0[l],
            p0[l],
            p0[l + 1] if l < L - 1 else None,
            p0[l - 1] if l else None,
            above,
            below,
            next_row,
            next_col,
        )
        bottom = storage[l] + next_row + shift_rows(next_row, 1)
        bottom = bottom + next_col + shift_columns(next_col, 1)
        if l:
            bottom = bottom + below
        if l < L - 1:
            bottom = bottom + above
        diag[l] = bottom
        face[0, l] = above if l < L - 1 else jnp.zeros((R, C), F32)
        face[1, l] = next_row
        face[2, l] = next_col
        below = above

    for side in SIDES:
        k = 15 - near_end(side)
        normal, along = (1, 0) if side < 2 else (0, 1)
        for n, ref in enumerate((p0, total, trans.at[normal], num, diag)):
            near_out[side, 16 * n : 16 * n + 16] = plane(ref, side, k)
        if side < 2:
            for h in (0, 1):
                perf_out[side, 8 + h : 9 + h] = trans[
                    along, L - 1, k : k + 1, 128 * h : 128 * h + 128
                ]
        else:
            near_out[side, 80:81] = trans[along, k, R - 1 : R, :]
        for n, ref in enumerate((face.at[along], face.at[2], frac)):
            bulk_out[side, 16 * n : 16 * n + 16] = plane(ref, side, k)
    for c in range(4):
        k, m = 15 - 15 * (c // 2), 15 - 15 * (c % 2)
        for n, ref in enumerate((p0, total, trans.at[0], trans.at[1], diag)):
            corner_out[c, n : n + 1] = ref[m, k : k + 1, :]

    for n in (5, 6, 9):
        loads[n].wait()
    field = total[...].reshape(L * R, C)
    parts = split(field * p0[...].reshape(L * R, C)) + split(field)
    picked = jnp.dot(
        jnp.concatenate(parts, axis=0), column_hot[...], preferred_element_type=F32
    )
    place = lax.broadcasted_iota(jnp.int32, (L * R, 128), 0)
    sums = []
    for n in (0, 1):
        part = jnp.zeros((1, 128), F32)
        for g in range(GROUPS):
            pair = picked[2 * n * L * R : 2 * (n + 1) * L * R, 128 * g : 128 * g + 128]
            chosen = jnp.where(place == own_row[g], pair[0 : L * R] + pair[L * R :], 0.0)
            part = part + own_index[g] * jnp.sum(chosen, axis=0, keepdims=True)
        part = part + pltpu.roll(part, 64, 1)
        sums.append(part + pltpu.roll(part, 32, 1))
    quarter = lax.broadcasted_iota(jnp.int32, (1, 128), 1) // WELLS
    packed = jnp.where(quarter == 0, sums[0], sums[1])
    packed = jnp.where(quarter == 2, four(tgt[...]), packed)
    packed = jnp.where(quarter == 3, four(ctl[...].astype(F32)), packed)
    tile_out[...] = packed
    tiles[4 + gz] = packed

    pl.semaphore_wait(
        barrier, count_z * (1 + has[0].astype(jnp.int32) + has[1].astype(jnp.int32)) - 1
    )

    def target(side):
        step = 1 - 2 * (side % 2)
        return (gx + step, gz) if side < 2 else (gx, gz + step)

    def remote(src, dst, send, recv, device):
        return pltpu.make_async_remote_copy(
            src_ref=src,
            dst_ref=dst,
            send_sem=send_sem.at[send],
            recv_sem=recv_sem.at[recv],
            device_id=device,
            device_id_type=MESH,
        )

    front, near, perf, bulk, last = [], [], [], [], []
    for c in range(4):
        s, t = c // 2, 2 + c % 2
        ok = (has[s ^ 1] & has[t ^ 1], has[s] & has[t])
        to = (target(s)[0], target(t)[1])
        near.append((*ok, remote(corner_out.at[c], corner_in.at[c], 4 + c, 4 + c, to)))
        last.append((*ok, remote(last_corner_out.at[c], last_corner_in.at[c], 4 + c, 18 + c, to)))
    for side in SIDES:
        ok, to = (has[side ^ 1], has[side]), target(side)
        rows = pl.ds(0, (48, 32, 88, 88)[side])
        copy = remote(near_out.at[side, rows], near_in.at[side, rows], side, side, to)
        (front if side < 2 else near).append((*ok, copy))
        if side < 2:
            rows = pl.ds(48, 32)
            copy = remote(
                near_out.at[side, rows], near_in.at[side, rows], 13 + side, 25 + side, to
            )
            near.append((*ok, copy))
        bulk.append((*ok, remote(bulk_out.at[side], bulk_in.at[side], 15 + side, 10 + side, to)))
        last.append((*ok, remote(last_out.at[side], last_in.at[side], 19 + side, 14 + side, to)))
    for side in (0, 1):
        ok, to = (has[side ^ 1], has[side]), target(side)
        perf.append((*ok, remote(perf_out.at[side], perf_in.at[side], 8 + side, 8 + side, to)))

    def start(copies):
        for out, _, copy in copies:

            @pl.when(out)
            def _():
                copy.start()

    def arrive(copies):
        for _, came, copy in copies:

            @pl.when(came)
            def _():
                copy.wait_recv()

    def sent(copies):
        for out, _, copy in copies:

            @pl.when(out)
            def _():
                copy.wait_send()

    def tile_copy(dx, z_from, z_to):
        return pltpu.make_async_remote_copy(
            src_ref=tile_out,
            dst_ref=tiles.at[4 * (1 - dx) + z_from],
            send_sem=send_sem.at[11 - dx],
            recv_sem=recv_sem.at[23 - dx],
            device_id=(gx + dx, z_to),
            device_id_type=MESH,
        )

    start(perf)
    ties = []
    for dx in (1, -1, 0):
        for z in range(4):
            if dx:
                ok = (has[1 if dx > 0 else 0], has[0 if dx > 0 else 1])
            else:
                ok = (gz != z, gz != z)
            ties.append((*ok, dx, z))
    for out, _, dx, z in ties:

        @pl.when(out)
        def _():
            tile_copy(dx, gz, z).start()

    start(front)
    start(near)


    def stacked(values):
        return jnp.concatenate(split(values), axis=0)

    def halves(values):
        n = values.shape[0] // 2
        return values[0:n] + values[n:]

    own_flat = jnp.concatenate(own_index, axis=1)
    columns_own[...] = jnp.concatenate([one_hot(C, c) for c in own_column], axis=1).T.astype(BF16)

    def own_scatter(values):
        high, low = split(values)
        rows = jnp.concatenate([own_hot[...] * high, own_hot[...] * low], axis=0)
        found = jnp.dot(rows, columns_own[...], preferred_element_type=F32)
        return halves(found).reshape(L + 2, R, C)

    index_sum[...] = own_scatter(own_flat)
    def group_wait(dx, sem):
        some = tiles.at[pl.ds(0, 4 if dx else 3)]
        pltpu.make_async_copy(some, some, sem).wait()

    def bottoms(groups):
        parts = [[tiles[4 * group + z] for z in range(4)] for group in groups]
        tile = jnp.concatenate([a + b + c + d for a, b, c, d in parts], axis=0)
        given = jnp.concatenate([group[0] for group in parts], axis=0)
        aim, mode = pltpu.roll(given, 64, 1), pltpu.roll(given, 32, 1)
        bottom = jnp.where(mode == 0.0, (aim + tile) / pltpu.roll(tile, 96, 1), aim)
        quarter = lax.broadcasted_iota(jnp.int32, bottom.shape, 1) // WELLS
        bottom = jnp.where(quarter == 0, bottom, 0.0)
        bottom = bottom + pltpu.roll(bottom, 64, 1)
        bottom = bottom + pltpu.roll(bottom, 32, 1)
        return jnp.concatenate([bottom] * GROUPS, axis=1)

    group_wait(0, recv_sem.at[23])

    bottom = bottoms([1])
    hole[...] = bottom[:, 0:WELLS]
    own_source[...] = own_scatter(own_flat * bottom)

    for l in range(L):
        src = total[l] * (own_source[l] - p0[l] * index_sum[l])
        over = 1.0 / diag[l]
        value = num[l] + src
        source[l] = src
        rhs[l] = storage[l] * p0[l] + src
        num[l] = value
        inverse[l] = over
        first[l] = value * over

    arrive(perf)
    start(bulk)

    side_rates = []
    for side in (0, 1):
        cell = [perf_in[side, g : g + 1].astype(jnp.int32) for g in range(GROUPS)]
        index = [perf_in[side, GROUPS + g : GROUPS + g + 1] for g in range(GROUPS)]
        rates = [one_hot(L, side_rows(v, gz, side)) * i for v, i in zip(cell, index)]
        side_rates.append(jnp.concatenate(rates, axis=1))
        for g in range(GROUPS):
            part = slice(128 * g, 128 * g + 128)
            side_columns[side, :, part] = one_hot(C, cell_parts(cell[g], gz)[2]).astype(BF16)

    for dx in (1, -1):

        @pl.when(has[0 if dx > 0 else 1])
        def _():
            group_wait(dx, recv_sem.at[23 - dx])

    bottom = bottoms([0, 2])
    for side in (0, 1):
        rates = side_rates[side]
        found = lax.dot_general(
            side_columns[side],
            stacked(jnp.concatenate([rates, rates * bottom[side : side + 1]], axis=0)),
            (((1,), (1,)), ((), ())),
            preferred_element_type=F32,
        )
        found = halves(found.T)
        side_index[side] = found[0:L]
        side_source[side] = found[L:]

    arrive(front)
    arrive(near[-2:])

    for side in SIDES:
        k = near_end(side)
        across = planes(near_in, side, 2)
        if side % 2:
            across = plane(trans.at[1 if side < 2 else 0], side, k)
        rate = plane(total, side, k) + planes(near_in, side, 1)
        rate = rate * across * jnp.where(has[side], 0.5, 0.0)
        border[side] = rate
        add_to_plane(diag, side, k, rate)
        add_to_plane(num, side, k, rate * planes(near_in, side, 0))

    for side in SIDES:
        k = near_end(side)
        over = 1.0 / plane(diag, side, k)
        set_plane(inverse, side, k, over)
        set_plane(first, side, k, plane(num, side, k) * over)
        weight[side] = border[side] * over

    for l in range(L):
        second[l] = sweep_layer(first, rhs, face, l) * inverse[l]

    arrive(near[:-2])

    for side in SIDES:
        k = near_end(side)
        p, here = planes(near_in, side, 0), planes(near_in, side, 1)
        if side < 2:
            well, index = side_source[side], side_index[side]
        else:
            n = L + 1 if side == 2 else L
            well, index = own_source[n], index_sum[n]
        value = planes(near_in, side, 3) + border[side] * plane(p0, side, k)
        ring[side] = value + here * (well - p * index)
        over_ring[side] = planes(near_in, side, 4) + border[side]
        for e, at, c in ends(side):
            cell = corner_in[c]
            if e and side < 2:
                rate = jnp.concatenate([perf_in[side, 8:9], perf_in[side, 9:10]], axis=1)
            elif e:
                rate = near_in[side, 80:81]
            else:
                rate = cell[2:3] if side < 2 else cell[3:4]
            rate = rate * jnp.where(has[c // 2] & has[2 + c % 2], 0.5, 0.0)
            rate = rate * (near_in[side, 16 + at : 17 + at] + cell[1:2])
            end_face[2 * side + e] = rate
            ring[side, at : at + 1] += rate * cell[0:1]
            over_ring[side, at : at + 1] += rate
        over_ring[side] = 1.0 / over_ring[side]
        add_to_plane(second, side, k, weight[side] * (ring[side] * over_ring[side]))
    for c in range(4):
        s, t = c // 2, c % 2
        over_corner[c] = 1.0 / (
            corner_in[c, 4:5] + end_face[2 * s + t] + end_face[2 * (2 + t) + s]
        )

    for l in range(L):
        value = sweep_layer(second, rhs, face, l)
        num[l] = value
        third[l] = value * inverse[l]

    for side in SIDES:
        k = 15 - near_end(side)
        behind = 14 if k else 1
        across = plane(face.at[1 if side < 2 else 0], side, min(k, 14))
        last_out[side, 0:16] = plane(second, side, k)
        last_out[side, 16:32] = plane(num, side, k)
        last_out[side, 32:48] = plane(rhs, side, k) + across * plane(third, side, behind)
        for e in (0, 1):
            other = 2 + e if side < 2 else e
            last_out[side, 48 + e : 49 + e] = (
                weight[other, behind : behind + 1] * across[15 * e : 15 * e + 1]
            )
    for c in range(4):
        k, m = 15 - 15 * (c // 2), 15 - 15 * (c % 2)
        k2, m2 = 14 if k else 1, 14 if m else 1
        last_corner_out[c, 0:1] = second[m, k : k + 1, :]
        last_corner_out[c, 1:2] = num[m, k : k + 1, :]
        last_corner_out[c, 2:3] = second[m, k2 : k2 + 1, :]
        last_corner_out[c, 3:4] = second[m2, k : k + 1, :]
    sent(front)
    sent(near)
    start(last)

    for l in range(L):
        fourth[l] = sweep_layer(third, rhs, face, l) * inverse[l]

    for l in range(L):
        src, part = source[l], frac[l]
        gas_source = jnp.maximum(src, 0.0) + jnp.minimum(src, 0.0) * part
        source[l] = local[0, l] + local[2, l] * gas_source
        frac_next[0, l] = shift_rows(part, -1)
        frac_next[1, l] = shift_columns(part, -1)

    sent(perf)
    for dx in (1, -1, 0):
        out = True if dx == 0 else has[1 if dx > 0 else 0]

        @pl.when(out)
        def _():
            group_wait(dx, send_sem.at[11 - dx])

    arrive(bulk)
    sent(bulk)


    arrive(last)
    sent(last)


def solve(
    storage,
    local,
    frac,
    frac_next,
    face,
    inverse,
    rhs,
    source,
    second,
    third,
    fourth,
    border,
    weight,
    over_ring,
    end_face,
    over_corner,
    bulk_in,
    bulk_out,
    last_in,
    last_corner_in,
    hole,
    new_p,
    residual,
    new_s,
    new_h,
    new_hole,
    flows,
    out_r,
    out_s,
    out_h,
    sems,
):
    new_hole[...] = hole[...]
    spot = lax.broadcasted_iota(jnp.int32, (16, C), 0)
    corners = []
    for c in range(4):
        s, t = c // 2, c % 2
        value = last_corner_in[c, 1:2]
        value = value + end_face[2 * s + t] * last_in[s, 15 * t : 15 * t + 1]
        value = value + end_face[2 * (2 + t) + s] * last_in[2 + t, 15 * s : 15 * s + 1]
        corners.append(value * over_corner[c])
    rings, parts = [], []
    for side in SIDES:
        k = near_end(side)
        rate = border[side]
        value = planes(last_in, side, 1) + rate * plane(second, side, k)
        add = planes(last_in, side, 2)
        for e, at, c in ends(side):
            cell = last_corner_in[c]
            value = value + jnp.where(spot == at, end_face[2 * side + e] * cell[0:1], 0.0)
            far = cell[2:3] if side < 2 else cell[3:4]
            add = add + jnp.where(spot == at, last_in[side, 48 + e : 49 + e] * far, 0.0)
            add = add + jnp.where(spot == at, end_face[2 * side + e] * corners[c], 0.0)
        value = value * over_ring[side]
        rings.append(value)
        along, col = planes(bulk_in, side, 0), planes(bulk_in, side, 1)
        parts.append(inner_sum(add, value, None, None, None, None, along, col))
    for side in SIDES:
        k = near_end(side)
        behind = 14 if k else 1
        change = weight[side] * planes(last_in, side, 0)
        add_to_plane(third, side, k, change)
        along, col = planes(bulk_out, side ^ 1, 0), planes(bulk_out, side ^ 1, 1)
        across = plane(face.at[1 if side < 2 else 0], side, min(k, 14))
        value = inner_sum(border[side] * rings[side], change, None, None, None, None, along, col)
        add_to_plane(fourth, side, k, value * plane(inverse, side, k))
        add_to_plane(fourth, side, behind, across * change * plane(inverse, side, behind))

    writes = [pltpu.make_async_copy(fourth, new_p, sems.at[0, 3])]
    writes[0].start()
    for side in SIDES:
        k = near_end(side)
        outer = (parts[side] + border[side] * plane(third, side, k)) * over_ring[side]
        rate = -border[side] if side == 0 else border[side]
        flow = rate * (plane(fourth, side, k) - outer)
        flows[side, 0] = flow
        flows[side, 1] = flow * jnp.where(
            (flow < 0) if side == 0 else (flow > 0),
            planes(bulk_out, side ^ 1, 2),
            planes(bulk_in, side, 2),
        )

    first_row, last_row = spot == 0, spot == R - 1
    below = gas_below = None
    for l in range(L):
        p, part = fourth[l], frac[l]
        flow = face[1, l] * (p - shift_rows(p, -1))
        gas = flow * jnp.where(flow > 0, part, frac_next[0, l])
        flow = jnp.where(last_row, flows[1, 0, l : l + 1], flow)
        gas = jnp.where(last_row, flows[1, 1, l : l + 1], gas)
        net = flow - jnp.where(first_row, flows[0, 0, l : l + 1], shift_rows(flow, 1))
        out = gas - jnp.where(first_row, flows[0, 1, l : l + 1], shift_rows(gas, 1))
        flow = face[2, l] * (p - shift_columns(p, -1))
        gas = flow * jnp.where(flow > 0, part, frac_next[1, l])
        net = net + flow - shift_columns(flow, 1)
        out = out + gas - shift_columns(gas, 1)
        if l:
            net, out = net - below, out - gas_below
        else:
            net, out = net + flows[2, 0], out + flows[2, 1]
        if l < L - 1:
            below = face[0, l] * (p - fourth[l + 1])
            gas_below = below * jnp.where(below > 0, part, frac[l + 1])
        else:
            below, gas_below = flows[3, 0], flows[3, 1]
        net, out = net + below, out + gas_below
        out_r[l] = rhs[l] - storage[l] * p - net
        saturation = source[l] - local[2, l] * out
        out_s[l] = saturation
        out_h[l] = jnp.maximum(local[1, l], saturation)
        if l % 8 == 7:
            part = pl.ds(l - 7, 8)
            for n, (src, dst) in enumerate(
                ((out_r, residual), (out_s, new_s), (out_h, new_h))
            ):
                copy = pltpu.make_async_copy(src.at[part], dst.at[part], sems.at[l // 8, n])
                copy.start()
                writes.append(copy)
    for copy in writes:
        copy.wait()


def body(
    count_x,
    count_z,
    pressure,
    saturation,
    sat_history,
    storage,
    step_volume,
    transmiss,
    perf_cell,
    perf_index,
    control,
    target,
):
    vmem = pl.BlockSpec(memory_space=pltpu.VMEM)
    hbm = pl.BlockSpec(memory_space=pltpu.HBM)
    dma = pltpu.SemaphoreType.DMA
    block = (L, R, C)
    side = (4, 16, C)
    mid = pl.pallas_call(
        functools.partial(exchange, count_x, count_z),
        out_shape=[
            pltpu.VMEM(shape, F32)
            for shape in (
                block,
                (3, *block),
                block,
                (2, *block),
                (3, *block),
                *[block] * 6,
                *[side] * 3,
                (8, 1, C),
                (4, 1, C),
                *[(4, 48, C)] * 2,
                (4, 56, C),
                (4, 4, C),
                (1, WELLS),
            )
        ],
        in_specs=[hbm] * 10,
        out_specs=[vmem] * 21,
        scratch_shapes=[
            pltpu.VMEM(block, F32),
            pltpu.VMEM(block, F32),
            pltpu.VMEM((3, *block), F32),
            *[pltpu.VMEM(block, F32)] * 3,
            pltpu.VMEM(side, F32),
            pltpu.VMEM((L + 2, R, C), F32),
            pltpu.VMEM((2, L, C), F32),
            pltpu.VMEM((L + 2, R, C), F32),
            pltpu.VMEM((2, L, C), F32),
            pltpu.VMEM(((L + 2) * R, 512), BF16),
            pltpu.VMEM((C, 512), BF16),
            pltpu.VMEM((512, C), BF16),
            pltpu.VMEM((2, C, 512), BF16),
            *[pltpu.VMEM((4, 88, C), F32)] * 2,
            *[pltpu.VMEM((4, 5, C), F32)] * 2,
            pltpu.VMEM((4, 56, C), F32),
            pltpu.VMEM((4, 4, C), F32),
            *[pltpu.VMEM((2, 16, 128), F32)] * 2,
            pltpu.VMEM((1, 128), F32),
            pltpu.VMEM((12, 1, 128), F32),
            pltpu.VMEM((NP, WELLS), jnp.int32),
            pltpu.VMEM((NP, WELLS), F32),
            pltpu.VMEM((1, WELLS), jnp.int32),
            pltpu.VMEM((1, WELLS), F32),
            dma((23,)),
            dma((27,)),
        ],
        compiler_params=pltpu.CompilerParams(
            collective_id=0, has_side_effects=True, vmem_limit_bytes=VMEM_LIMIT
        ),
        name="exchange",
    )(
        *[
            pltpu.with_memory_space_constraint(values, pltpu.HBM)
            for values in (
                pressure,
                saturation,
                sat_history,
                storage,
                step_volume,
                transmiss,
                perf_cell.T,
                perf_index.T,
                control.reshape(1, WELLS),
                target.reshape(1, WELLS),
            )
        ]
    )
    *fields, hole = pl.pallas_call(
        solve,
        out_shape=[jax.ShapeDtypeStruct(block, F32)] * 4
        + [jax.ShapeDtypeStruct((1, WELLS), F32)],
        in_specs=[vmem] * 21,
        out_specs=[hbm] * 4 + [vmem],
        scratch_shapes=[
            pltpu.VMEM((4, 2, 16, C), F32),
            *[pltpu.VMEM(block, F32)] * 3,
            dma((2, 4)),
        ],
        compiler_params=pltpu.CompilerParams(vmem_limit_bytes=VMEM_LIMIT),
        name="solve",
    )(*mid)
    return (*fields, hole.reshape(WELLS))


def solution(mesh):
    cells = P("gz", "gx", None)
    return jax.shard_map(
        functools.partial(body, mesh.shape["gx"], mesh.shape["gz"]),
        mesh=mesh,
        in_specs=(
            *[cells] * 5,
            P(None, "gz", "gx", None),
            P("gx", None),
            P("gx", None),
            P("gx"),
            P("gx"),
        ),
        out_specs=(*[cells] * 4, P("gx")),
        check_vma=False,
    )
```

```python
import functools

import jax
import jax.numpy as jnp
from jax import lax
from jax.experimental import pallas as pl
from jax.experimental.pallas import tpu as pltpu
from jax.sharding import PartitionSpec as P

L = 16
R = 16
C = 256
WELLS = 32
NP = 16
GROUPS = WELLS * NP // 128
SIDES = range(4)
MESH = pl.DeviceIdType.MESH
F32 = jnp.float32
BF16 = jnp.bfloat16
VMEM_LIMIT = 26 * 2**20


def mobility(sat, history):
    trapped = history / (1.0 + 1.5 * history)
    excess = jnp.maximum(sat - trapped, 0.0)
    free_gas = 0.5 * (excess + jnp.sqrt(excess * excess + excess / 0.375))
    relperm = jnp.where(sat < history, free_gas * free_gas, sat * sat)
    gas = relperm / 0.5
    total = (1.0 - sat) * (1.0 - sat) + gas
    return (total, gas / total)


def split(values):
    high = values.astype(BF16)
    low = (values - high.astype(F32)).astype(BF16)
    return high, low


def four(row):
    return jnp.concatenate([row, row, row, row], axis=1)


def lane_groups(table):
    wide = four(table)
    place = lax.broadcasted_iota(jnp.int32, (1, 128), 1) // WELLS
    rows = []
    for g in range(GROUPS):
        row = wide[4 * g : 4 * g + 1]
        for k in range(1, 4):
            row = jnp.where(place == k, wide[4 * g + k : 4 * g + k + 1], row)
        rows.append(row)
    return rows


def cell_parts(cell, gz):
    layer = lax.shift_right_logical(cell, 12) - gz * L
    return layer, lax.shift_right_logical(cell, 8) & (R - 1), cell & (C - 1)


def one_hot(size, target):
    return jnp.where(lax.broadcasted_iota(jnp.int32, (size, 128), 0) == target, 1.0, 0.0)


def own_rows(cell, gz):
    layer, row, _ = cell_parts(cell, gz)
    index = jnp.where(layer == -1, L + 1, layer)
    return jnp.where((layer >= -1) & (layer <= L), index * R + row, -1)


def side_rows(cell, gz, side):
    layer, row, _ = cell_parts(cell, gz)
    return jnp.where((layer >= 0) & (layer < L) & (row == (0 if side else R - 1)), layer, -1)


def shift_rows(value, by):
    return pltpu.roll(value, by % value.shape[0], 0)


def shift_columns(value, by):
    return pltpu.roll(value, by % C, 1)


def near_end(side):
    return 15 * (side % 2)


def plane(ref, side, k):
    return ref[0:L, k, :] if side < 2 else ref[k, 0:R, :]


def add_to_plane(ref, side, k, value):
    if side < 2:
        ref[0:L, k, :] += value
    else:
        ref[k, 0:R, :] += value


def set_plane(ref, side, k, value):
    if side < 2:
        ref[0:L, k, :] = value
    else:
        ref[k, 0:R, :] = value


def ends(side):
    for e in (0, 1):
        yield e, 15 * e, 2 * side + e if side < 2 else 2 * e + side - 2


def planes(ref, side, n):
    return ref[side, 16 * n : 16 * n + 16]


def inner_sum(start, p, up, down, above, below, next_row, next_col):
    value = start + next_row * shift_rows(p, -1) + shift_rows(next_row * p, 1)
    value = value + next_col * shift_columns(p, -1) + shift_columns(next_col * p, 1)
    if up is not None:
        value = value + above * up
    if down is not None:
        value = value + below * down
    return value


def sweep_layer(ref, rhs, face, l):
    return inner_sum(
        rhs[l],
        ref[l],
        ref[l + 1] if l < L - 1 else None,
        ref[l - 1] if l else None,
        face[0, l],
        face[0, l - 1] if l else None,
        face[1, l],
        face[2, l],
    )


def exchange(
    count_x,
    count_z,
    p_in,
    sat_in,
    hist_in,
    sto_in,
    vol_in,
    tr_in,
    pc_in,
    pi_in,
    ctl_in,
    tgt_in,
    storage,
    local,
    frac,
    frac_next,
    face,
    inverse,
    rhs,
    source,
    second,
    third,
    fourth,
    border,
    weight,
    over_ring,
    end_face,
    over_corner,
    bulk_in,
    bulk_out,
    mid_in,
    last_in,
    last_corner_in,
    hole,
    p0,
    total,
    trans,
    num,
    diag,
    first,
    ring,
    index_sum,
    side_index,
    own_source,
    side_source,
    own_hot,
    column_hot,
    columns_own,
    side_columns,
    near_out,
    near_in,
    corner_out,
    corner_in,
    mid_out,
    last_out,
    last_corner_out,
    perf_out,
    perf_in,
    tile_out,
    tiles,
    pc,
    pi,
    ctl,
    tgt,
    send_sem,
    recv_sem,
):
    gx, gz = lax.axis_index("gx"), lax.axis_index("gz")
    has = (gx > 0, gx < count_x - 1, gz > 0, gz < count_z - 1)

    barrier = pltpu.get_barrier_semaphore()

    def signal_column(x):
        def one(z, carry):
            pl.semaphore_signal(barrier, inc=1, device_id=(x, z), device_id_type=MESH)
            return carry

        return one

    def others(z, carry):
        @pl.when(z != gz)
        def _():
            pl.semaphore_signal(barrier, inc=1, device_id=(gx, z), device_id_type=MESH)

        return carry

    for s in (0, 1):

        @pl.when(has[s])
        def _():
            lax.fori_loop(0, count_z, signal_column(gx + 2 * s - 1), 0)

    lax.fori_loop(0, count_z, others, 0)

    loads = [
        pltpu.make_async_copy(pc_in, pc, send_sem.at[0]),
        pltpu.make_async_copy(pi_in, pi, send_sem.at[1]),
        pltpu.make_async_copy(sat_in, local.at[0], send_sem.at[2]),
        pltpu.make_async_copy(hist_in, local.at[1], send_sem.at[3]),
        pltpu.make_async_copy(p_in, p0, send_sem.at[4]),
        pltpu.make_async_copy(ctl_in, ctl, send_sem.at[5]),
        pltpu.make_async_copy(tgt_in, tgt, send_sem.at[6]),
        pltpu.make_async_copy(tr_in, trans, send_sem.at[7]),
        pltpu.make_async_copy(sto_in, storage, send_sem.at[8]),
        pltpu.make_async_copy(vol_in, local.at[2], send_sem.at[9]),
    ]
    for copy in loads:
        copy.start()

    for side in SIDES:

        @pl.when(jnp.logical_not(has[side]))
        def _():
            near_in[side] = jnp.zeros((88, C), F32)
            near_in[side, 64:80] = jnp.ones((16, C), F32)
            bulk_in[side] = jnp.zeros((48, C), F32)
            mid_in[side] = jnp.zeros((24, C), F32)
            last_in[side] = jnp.zeros((32, C), F32)
            if side < 2:
                perf_in[side] = jnp.where(
                    lax.broadcasted_iota(jnp.int32, (16, 128), 0) < GROUPS, 1e9, 0.0
                )
                tiles[8 * side : 8 * side + 4] = jnp.ones((4, 1, 128), F32)

    for c in range(4):

        @pl.when(jnp.logical_not(has[c // 2] & has[2 + c % 2]))
        def _():
            corner_in[c] = jnp.zeros((5, C), F32)
            corner_in[c, 4:5] = jnp.ones((1, C), F32)
            last_corner_in[c] = jnp.zeros((4, C), F32)

    for n in (0, 1):
        loads[n].wait()
    cell = lane_groups(pc[...])
    own_index = lane_groups(pi[...])
    own_column = [cell_parts(v, gz)[2] for v in cell]
    own_row = [own_rows(v, gz) for v in cell]
    for g in range(GROUPS):
        part = slice(128 * g, 128 * g + 128)
        own_hot[:, part] = one_hot((L + 2) * R, own_row[g]).astype(BF16)
        column_hot[:, part] = one_hot(C, own_column[g]).astype(BF16)
    for side in (0, 1):
        for g in range(GROUPS):
            perf_out[side, g : g + 1] = cell[g].astype(F32)
            perf_out[side, GROUPS + g : GROUPS + g + 1] = own_index[g]

    for n in (2, 3):
        loads[n].wait()
    for l in range(L):
        total[l], frac[l] = mobility(local[0, l], local[1, l])
    for n in (4, 7, 8):
        loads[n].wait()

    row = lax.broadcasted_iota(jnp.int32, (R, C), 0)
    column = lax.broadcasted_iota(jnp.int32, (R, C), 1)
    row_half = jnp.where(row == R - 1, 0.0, 0.5)
    column_half = jnp.where(column == C - 1, 0.0, 0.5)
    below = None
    for l in range(L):
        here = total[l]
        next_row = trans[1, l] * row_half * (here + shift_rows(here, -1))
        next_col = trans[2, l] * column_half * (here + shift_columns(here, -1))
        above = trans[0, l] * 0.5 * (here + total[l + 1]) if l < L - 1 else None
        num[l] = inner_sum(
            storage[l] * p0[l],
            p0[l],
            p0[l + 1] if l < L - 1 else None,
            p0[l - 1] if l else None,
            above,
            below,
            next_row,
            next_col,
        )
        bottom = storage[l] + next_row + shift_rows(next_row, 1)
        bottom = bottom + next_col + shift_columns(next_col, 1)
        if l:
            bottom = bottom + below
        if l < L - 1:
            bottom = bottom + above
        diag[l] = bottom
        face[0, l] = above if l < L - 1 else jnp.zeros((R, C), F32)
        face[1, l] = next_row
        face[2, l] = next_col
        below = above

    for side in SIDES:
        k = 15 - near_end(side)
        normal, along = (1, 0) if side < 2 else (0, 1)
        for n, ref in enumerate((p0, total, trans.at[normal], num, diag)):
            near_out[side, 16 * n : 16 * n + 16] = plane(ref, side, k)
        if side < 2:
            for h in (0, 1):
                perf_out[side, 8 + h : 9 + h] = trans[
                    along, L - 1, k : k + 1, 128 * h : 128 * h + 128
                ]
        else:
            near_out[side, 80:81] = trans[along, k, R - 1 : R, :]
        for n, ref in enumerate((face.at[along], face.at[2], frac)):
            bulk_out[side, 16 * n : 16 * n + 16] = plane(ref, side, k)
    for c in range(4):
        k, m = 15 - 15 * (c // 2), 15 - 15 * (c % 2)
        for n, ref in enumerate((p0, total, trans.at[0], trans.at[1], diag)):
            corner_out[c, n : n + 1] = ref[m, k : k + 1, :]

    for n in (5, 6, 9):
        loads[n].wait()
    field = total[...].reshape(L * R, C)
    parts = split(field * p0[...].reshape(L * R, C)) + split(field)
    picked = jnp.dot(
        jnp.concatenate(parts, axis=0), column_hot[...], preferred_element_type=F32
    )
    place = lax.broadcasted_iota(jnp.int32, (L * R, 128), 0)
    sums = []
    for n in (0, 1):
        part = jnp.zeros((1, 128), F32)
        for g in range(GROUPS):
            pair = picked[2 * n * L * R : 2 * (n + 1) * L * R, 128 * g : 128 * g + 128]
            chosen = jnp.where(place == own_row[g], pair[0 : L * R] + pair[L * R :], 0.0)
            part = part + own_index[g] * jnp.sum(chosen, axis=0, keepdims=True)
        part = part + pltpu.roll(part, 64, 1)
        sums.append(part + pltpu.roll(part, 32, 1))
    quarter = lax.broadcasted_iota(jnp.int32, (1, 128), 1) // WELLS
    packed = jnp.where(quarter == 0, sums[0], sums[1])
    packed = jnp.where(quarter == 2, four(tgt[...]), packed)
    packed = jnp.where(quarter == 3, four(ctl[...].astype(F32)), packed)
    tile_out[...] = packed
    tiles[4 + gz] = packed

    pl.semaphore_wait(
        barrier, count_z * (1 + has[0].astype(jnp.int32) + has[1].astype(jnp.int32)) - 1
    )

    def target(side):
        step = 1 - 2 * (side % 2)
        return (gx + step, gz) if side < 2 else (gx, gz + step)

    def remote(src, dst, send, recv, device):
        return pltpu.make_async_remote_copy(
            src_ref=src,
            dst_ref=dst,
            send_sem=send_sem.at[send],
            recv_sem=recv_sem.at[recv],
            device_id=device,
            device_id_type=MESH,
        )

    front, near, perf, bulk, mid, last = [], [], [], [], [], []
    for c in range(4):
        s, t = c // 2, 2 + c % 2
        ok = (has[s ^ 1] & has[t ^ 1], has[s] & has[t])
        to = (target(s)[0], target(t)[1])
        near.append((*ok, remote(corner_out.at[c], corner_in.at[c], 4 + c, 4 + c, to)))
        last.append((*ok, remote(last_corner_out.at[c], last_corner_in.at[c], 4 + c, 18 + c, to)))
    for side in SIDES:
        ok, to = (has[side ^ 1], has[side]), target(side)
        rows = pl.ds(0, (48, 32, 88, 88)[side])
        copy = remote(near_out.at[side, rows], near_in.at[side, rows], side, side, to)
        (front if side < 2 else near).append((*ok, copy))
        if side < 2:
            rows = pl.ds(48, 32)
            copy = remote(
                near_out.at[side, rows], near_in.at[side, rows], 13 + side, 25 + side, to
            )
            near.append((*ok, copy))
        bulk.append((*ok, remote(bulk_out.at[side], bulk_in.at[side], 15 + side, 10 + side, to)))
        mid.append((*ok, remote(mid_out.at[side], mid_in.at[side], side, 27 + side, to)))
        last.append((*ok, remote(last_out.at[side], last_in.at[side], 19 + side, 14 + side, to)))
    for side in (0, 1):
        ok, to = (has[side ^ 1], has[side]), target(side)
        perf.append((*ok, remote(perf_out.at[side], perf_in.at[side], 8 + side, 8 + side, to)))

    def start(copies):
        for out, _, copy in copies:

            @pl.when(out)
            def _():
                copy.start()

    def arrive(copies):
        for _, came, copy in copies:

            @pl.when(came)
            def _():
                copy.wait_recv()

    def sent(copies):
        for out, _, copy in copies:

            @pl.when(out)
            def _():
                copy.wait_send()

    def tile_copy(dx, z_from, z_to):
        return pltpu.make_async_remote_copy(
            src_ref=tile_out,
            dst_ref=tiles.at[4 * (1 - dx) + z_from],
            send_sem=send_sem.at[11 - dx],
            recv_sem=recv_sem.at[23 - dx],
            device_id=(gx + dx, z_to),
            device_id_type=MESH,
        )

    start(perf)
    ties = []
    for dx in (1, -1, 0):
        for z in range(4):
            if dx:
                ok = (has[1 if dx > 0 else 0], has[0 if dx > 0 else 1])
            else:
                ok = (gz != z, gz != z)
            ties.append((*ok, dx, z))
    for out, _, dx, z in ties:

        @pl.when(out)
        def _():
            tile_copy(dx, gz, z).start()

    start(front)
    start(near)


    def stacked(values):
        return jnp.concatenate(split(values), axis=0)

    def halves(values):
        n = values.shape[0] // 2
        return values[0:n] + values[n:]

    own_flat = jnp.concatenate(own_index, axis=1)
    columns_own[...] = jnp.concatenate([one_hot(C, c) for c in own_column], axis=1).T.astype(BF16)

    def own_scatter(values):
        high, low = split(values)
        rows = jnp.concatenate([own_hot[...] * high, own_hot[...] * low], axis=0)
        found = jnp.dot(rows, columns_own[...], preferred_element_type=F32)
        return halves(found).reshape(L + 2, R, C)

    index_sum[...] = own_scatter(own_flat)
    def group_wait(dx, sem):
        some = tiles.at[pl.ds(0, 4 if dx else 3)]
        pltpu.make_async_copy(some, some, sem).wait()

    def bottoms(groups):
        parts = [[tiles[4 * group + z] for z in range(4)] for group in groups]
        tile = jnp.concatenate([a + b + c + d for a, b, c, d in parts], axis=0)
        given = jnp.concatenate([group[0] for group in parts], axis=0)
        aim, mode = pltpu.roll(given, 64, 1), pltpu.roll(given, 32, 1)
        bottom = jnp.where(mode == 0.0, (aim + tile) / pltpu.roll(tile, 96, 1), aim)
        quarter = lax.broadcasted_iota(jnp.int32, bottom.shape, 1) // WELLS
        bottom = jnp.where(quarter == 0, bottom, 0.0)
        bottom = bottom + pltpu.roll(bottom, 64, 1)
        bottom = bottom + pltpu.roll(bottom, 32, 1)
        return jnp.concatenate([bottom] * GROUPS, axis=1)

    group_wait(0, recv_sem.at[23])

    bottom = bottoms([1])
    hole[...] = bottom[:, 0:WELLS]
    own_source[...] = own_scatter(own_flat * bottom)

    for l in range(L):
        src = total[l] * (own_source[l] - p0[l] * index_sum[l])
        over = 1.0 / diag[l]
        value = num[l] + src
        source[l] = src
        rhs[l] = storage[l] * p0[l] + src
        num[l] = value
        inverse[l] = over
        first[l] = value * over

    arrive(perf)
    start(bulk)

    side_rates = []
    for side in (0, 1):
        cell = [perf_in[side, g : g + 1].astype(jnp.int32) for g in range(GROUPS)]
        index = [perf_in[side, GROUPS + g : GROUPS + g + 1] for g in range(GROUPS)]
        rates = [one_hot(L, side_rows(v, gz, side)) * i for v, i in zip(cell, index)]
        side_rates.append(jnp.concatenate(rates, axis=1))
        for g in range(GROUPS):
            part = slice(128 * g, 128 * g + 128)
            side_columns[side, :, part] = one_hot(C, cell_parts(cell[g], gz)[2]).astype(BF16)

    for dx in (1, -1):

        @pl.when(has[0 if dx > 0 else 1])
        def _():
            group_wait(dx, recv_sem.at[23 - dx])

    bottom = bottoms([0, 2])
    for side in (0, 1):
        rates = side_rates[side]
        found = lax.dot_general(
            side_columns[side],
            stacked(jnp.concatenate([rates, rates * bottom[side : side + 1]], axis=0)),
            (((1,), (1,)), ((), ())),
            preferred_element_type=F32,
        )
        found = halves(found.T)
        side_index[side] = found[0:L]
        side_source[side] = found[L:]

    arrive(front)
    arrive(near[-2:])

    for side in SIDES:
        k = near_end(side)
        across = planes(near_in, side, 2)
        if side % 2:
            across = plane(trans.at[1 if side < 2 else 0], side, k)
        rate = plane(total, side, k) + planes(near_in, side, 1)
        rate = rate * across * jnp.where(has[side], 0.5, 0.0)
        border[side] = rate
        add_to_plane(diag, side, k, rate)
        add_to_plane(num, side, k, rate * planes(near_in, side, 0))

    for side in SIDES:
        k = near_end(side)
        over = 1.0 / plane(diag, side, k)
        set_plane(inverse, side, k, over)
        set_plane(first, side, k, plane(num, side, k) * over)
        weight[side] = border[side] * over

    for l in range(L):
        second[l] = sweep_layer(first, rhs, face, l) * inverse[l]

    arrive(near[:-2])

    for side in SIDES:
        k = near_end(side)
        p, here = planes(near_in, side, 0), planes(near_in, side, 1)
        if side < 2:
            well, index = side_source[side], side_index[side]
        else:
            n = L + 1 if side == 2 else L
            well, index = own_source[n], index_sum[n]
        value = planes(near_in, side, 3) + border[side] * plane(p0, side, k)
        ring[side] = value + here * (well - p * index)
        over_ring[side] = planes(near_in, side, 4) + border[side]
        for e, at, c in ends(side):
            cell = corner_in[c]
            if e and side < 2:
                rate = jnp.concatenate([perf_in[side, 8:9], perf_in[side, 9:10]], axis=1)
            elif e:
                rate = near_in[side, 80:81]
            else:
                rate = cell[2:3] if side < 2 else cell[3:4]
            rate = rate * jnp.where(has[c // 2] & has[2 + c % 2], 0.5, 0.0)
            rate = rate * (near_in[side, 16 + at : 17 + at] + cell[1:2])
            end_face[2 * side + e] = rate
            ring[side, at : at + 1] += rate * cell[0:1]
            over_ring[side, at : at + 1] += rate
        over_ring[side] = 1.0 / over_ring[side]
        add_to_plane(second, side, k, weight[side] * (ring[side] * over_ring[side]))
    for c in range(4):
        s, t = c // 2, c % 2
        over_corner[c] = 1.0 / (
            corner_in[c, 4:5] + end_face[2 * s + t] + end_face[2 * (2 + t) + s]
        )

    sent(front)
    sent(near)
    for side in SIDES:
        k = 15 - near_end(side)
        behind = 14 if k else 1
        across = plane(face.at[1 if side < 2 else 0], side, min(k, 14))
        mid_out[side, 0:16] = plane(second, side, k)
        for e in (0, 1):
            other = 2 + e if side < 2 else e
            mid_out[side, 16 + e : 17 + e] = (
                weight[other, behind : behind + 1] * across[15 * e : 15 * e + 1]
            )
    start(mid)

    for l in range(L):
        value = sweep_layer(second, rhs, face, l)
        num[l] = value
        third[l] = value * inverse[l]

    for side in SIDES:
        k = 15 - near_end(side)
        behind = 14 if k else 1
        across = plane(face.at[1 if side < 2 else 0], side, min(k, 14))
        last_out[side, 0:16] = plane(num, side, k)
        last_out[side, 16:32] = plane(rhs, side, k) + across * plane(third, side, behind)
    for c in range(4):
        k, m = 15 - 15 * (c // 2), 15 - 15 * (c % 2)
        k2, m2 = 14 if k else 1, 14 if m else 1
        last_corner_out[c, 0:1] = second[m, k : k + 1, :]
        last_corner_out[c, 1:2] = num[m, k : k + 1, :]
        last_corner_out[c, 2:3] = second[m, k2 : k2 + 1, :]
        last_corner_out[c, 3:4] = second[m2, k : k + 1, :]
    start(last)

    for l in range(L):
        fourth[l] = sweep_layer(third, rhs, face, l) * inverse[l]

    for l in range(L):
        src, part = source[l], frac[l]
        gas_source = jnp.maximum(src, 0.0) + jnp.minimum(src, 0.0) * part
        source[l] = local[0, l] + local[2, l] * gas_source
        frac_next[0, l] = shift_rows(part, -1)
        frac_next[1, l] = shift_columns(part, -1)

    sent(perf)
    for dx in (1, -1, 0):
        out = True if dx == 0 else has[1 if dx > 0 else 0]

        @pl.when(out)
        def _():
            group_wait(dx, send_sem.at[11 - dx])

    arrive(bulk)
    sent(bulk)


    arrive(mid)
    sent(mid)

    arrive(last)
    sent(last)


def solve(
    storage,
    local,
    frac,
    frac_next,
    face,
    inverse,
    rhs,
    source,
    second,
    third,
    fourth,
    border,
    weight,
    over_ring,
    end_face,
    over_corner,
    bulk_in,
    bulk_out,
    mid_in,
    last_in,
    last_corner_in,
    hole,
    new_p,
    residual,
    new_s,
    new_h,
    new_hole,
    flows,
    out_r,
    out_s,
    out_h,
    sems,
):
    writes = [pltpu.make_async_copy(hole, new_hole, sems.at[1, 3])]
    writes[0].start()
    spot = lax.broadcasted_iota(jnp.int32, (16, C), 0)
    corners = []
    for c in range(4):
        s, t = c // 2, c % 2
        value = last_corner_in[c, 1:2]
        value = value + end_face[2 * s + t] * mid_in[s, 15 * t : 15 * t + 1]
        value = value + end_face[2 * (2 + t) + s] * mid_in[2 + t, 15 * s : 15 * s + 1]
        corners.append(value * over_corner[c])
    rings, parts = [], []
    for side in SIDES:
        k = near_end(side)
        rate = border[side]
        value = planes(last_in, side, 0) + rate * plane(second, side, k)
        add = planes(last_in, side, 1)
        for e, at, c in ends(side):
            cell = last_corner_in[c]
            value = value + jnp.where(spot == at, end_face[2 * side + e] * cell[0:1], 0.0)
            far = cell[2:3] if side < 2 else cell[3:4]
            add = add + jnp.where(spot == at, mid_in[side, 16 + e : 17 + e] * far, 0.0)
            add = add + jnp.where(spot == at, end_face[2 * side + e] * corners[c], 0.0)
        value = value * over_ring[side]
        rings.append(value)
        along, col = planes(bulk_in, side, 0), planes(bulk_in, side, 1)
        parts.append(inner_sum(add, value, None, None, None, None, along, col))
    for side in SIDES:
        k = near_end(side)
        behind = 14 if k else 1
        change = weight[side] * planes(mid_in, side, 0)
        add_to_plane(third, side, k, change)
        along, col = planes(bulk_out, side ^ 1, 0), planes(bulk_out, side ^ 1, 1)
        across = plane(face.at[1 if side < 2 else 0], side, min(k, 14))
        value = inner_sum(border[side] * rings[side], change, None, None, None, None, along, col)
        add_to_plane(fourth, side, k, value * plane(inverse, side, k))
        add_to_plane(fourth, side, behind, across * change * plane(inverse, side, behind))

    writes.append(pltpu.make_async_copy(fourth, new_p, sems.at[0, 3]))
    writes[1].start()
    for side in SIDES:
        k = near_end(side)
        outer = (parts[side] + border[side] * plane(third, side, k)) * over_ring[side]
        rate = -border[side] if side == 0 else border[side]
        flow = rate * (plane(fourth, side, k) - outer)
        flows[side, 0] = flow
        flows[side, 1] = flow * jnp.where(
            (flow < 0) if side == 0 else (flow > 0),
            planes(bulk_out, side ^ 1, 2),
            planes(bulk_in, side, 2),
        )

    first_row, last_row = spot == 0, spot == R - 1
    below = gas_below = None
    for l in range(L):
        p, part = fourth[l], frac[l]
        flow = face[1, l] * (p - shift_rows(p, -1))
        gas = flow * jnp.where(flow > 0, part, frac_next[0, l])
        flow = jnp.where(last_row, flows[1, 0, l : l + 1], flow)
        gas = jnp.where(last_row, flows[1, 1, l : l + 1], gas)
        net = flow - jnp.where(first_row, flows[0, 0, l : l + 1], shift_rows(flow, 1))
        out = gas - jnp.where(first_row, flows[0, 1, l : l + 1], shift_rows(gas, 1))
        flow = face[2, l] * (p - shift_columns(p, -1))
        gas = flow * jnp.where(flow > 0, part, frac_next[1, l])
        net = net + flow - shift_columns(flow, 1)
        out = out + gas - shift_columns(gas, 1)
        if l:
            net, out = net - below, out - gas_below
        else:
            net, out = net + flows[2, 0], out + flows[2, 1]
        if l < L - 1:
            below = face[0, l] * (p - fourth[l + 1])
            gas_below = below * jnp.where(below > 0, part, frac[l + 1])
        else:
            below, gas_below = flows[3, 0], flows[3, 1]
        net, out = net + below, out + gas_below
        out_r[l] = rhs[l] - storage[l] * p - net
        saturation = source[l] - local[2, l] * out
        out_s[l] = saturation
        out_h[l] = jnp.maximum(local[1, l], saturation)
        if l % 8 == 7:
            part = pl.ds(l - 7, 8)
            for n, (src, dst) in enumerate(
                ((out_r, residual), (out_s, new_s), (out_h, new_h))
            ):
                copy = pltpu.make_async_copy(src.at[part], dst.at[part], sems.at[l // 8, n])
                copy.start()
                writes.append(copy)
    for copy in writes:
        copy.wait()


def body(
    count_x,
    count_z,
    pressure,
    saturation,
    sat_history,
    storage,
    step_volume,
    transmiss,
    perf_cell,
    perf_index,
    control,
    target,
):
    vmem = pl.BlockSpec(memory_space=pltpu.VMEM)
    hbm = pl.BlockSpec(memory_space=pltpu.HBM)
    dma = pltpu.SemaphoreType.DMA
    block = (L, R, C)
    side = (4, 16, C)
    mid = pl.pallas_call(
        functools.partial(exchange, count_x, count_z),
        out_shape=[
            pltpu.VMEM(shape, F32)
            for shape in (
                block,
                (3, *block),
                block,
                (2, *block),
                (3, *block),
                *[block] * 6,
                *[side] * 3,
                (8, 1, C),
                (4, 1, C),
                *[(4, 48, C)] * 2,
                (4, 24, C),
                (4, 32, C),
                (4, 4, C),
                (1, WELLS),
            )
        ],
        in_specs=[hbm] * 10,
        out_specs=[vmem] * 22,
        scratch_shapes=[
            pltpu.VMEM(block, F32),
            pltpu.VMEM(block, F32),
            pltpu.VMEM((3, *block), F32),
            *[pltpu.VMEM(block, F32)] * 3,
            pltpu.VMEM(side, F32),
            pltpu.VMEM((L + 2, R, C), F32),
            pltpu.VMEM((2, L, C), F32),
            pltpu.VMEM((L + 2, R, C), F32),
            pltpu.VMEM((2, L, C), F32),
            pltpu.VMEM(((L + 2) * R, 512), BF16),
            pltpu.VMEM((C, 512), BF16),
            pltpu.VMEM((512, C), BF16),
            pltpu.VMEM((2, C, 512), BF16),
            *[pltpu.VMEM((4, 88, C), F32)] * 2,
            *[pltpu.VMEM((4, 5, C), F32)] * 2,
            pltpu.VMEM((4, 24, C), F32),
            pltpu.VMEM((4, 32, C), F32),
            pltpu.VMEM((4, 4, C), F32),
            *[pltpu.VMEM((2, 16, 128), F32)] * 2,
            pltpu.VMEM((1, 128), F32),
            pltpu.VMEM((12, 1, 128), F32),
            pltpu.VMEM((NP, WELLS), jnp.int32),
            pltpu.VMEM((NP, WELLS), F32),
            pltpu.VMEM((1, WELLS), jnp.int32),
            pltpu.VMEM((1, WELLS), F32),
            dma((23,)),
            dma((31,)),
        ],
        compiler_params=pltpu.CompilerParams(
            collective_id=0, has_side_effects=True, vmem_limit_bytes=VMEM_LIMIT
        ),
        name="exchange",
    )(
        *[
            pltpu.with_memory_space_constraint(values, pltpu.HBM)
            for values in (
                pressure,
                saturation,
                sat_history,
                storage,
                step_volume,
                transmiss,
                perf_cell.T,
                perf_index.T,
                control.reshape(1, WELLS),
                target.reshape(1, WELLS),
            )
        ]
    )
    *fields, hole = pl.pallas_call(
        solve,
        out_shape=[jax.ShapeDtypeStruct(block, F32)] * 4
        + [jax.ShapeDtypeStruct((1, WELLS), F32)],
        in_specs=[vmem] * 22,
        out_specs=[hbm] * 5,
        scratch_shapes=[
            pltpu.VMEM((4, 2, 16, C), F32),
            *[pltpu.VMEM(block, F32)] * 3,
            dma((2, 4)),
        ],
        compiler_params=pltpu.CompilerParams(vmem_limit_bytes=VMEM_LIMIT),
        name="solve",
    )(*mid)
    return (*fields, hole.reshape(WELLS))


def solution(mesh):
    cells = P("gz", "gx", None)
    return jax.shard_map(
        functools.partial(body, mesh.shape["gx"], mesh.shape["gz"]),
        mesh=mesh,
        in_specs=(
            *[cells] * 5,
            P(None, "gz", "gx", None),
            P("gx", None),
            P("gx", None),
            P("gx"),
            P("gx"),
        ),
        out_specs=(*[cells] * 4, P("gx")),
        check_vma=False,
    )
```

```python
import functools

import jax
import jax.numpy as jnp
from jax import lax
from jax.experimental import pallas as pl
from jax.experimental.pallas import tpu as pltpu
from jax.sharding import PartitionSpec as P

L = 16
R = 16
C = 256
WELLS = 32
NP = 16
GROUPS = WELLS * NP // 128
SIDES = range(4)
MESH = pl.DeviceIdType.MESH
F32 = jnp.float32
BF16 = jnp.bfloat16
VMEM_LIMIT = 26 * 2**20


def mobility(sat, history):
    trapped = history / (1.0 + 1.5 * history)
    excess = jnp.maximum(sat - trapped, 0.0)
    free_gas = 0.5 * (excess + jnp.sqrt(excess * excess + excess / 0.375))
    relperm = jnp.where(sat < history, free_gas * free_gas, sat * sat)
    gas = relperm / 0.5
    total = (1.0 - sat) * (1.0 - sat) + gas
    return (total, gas / total)


def split(values):
    high = values.astype(BF16)
    low = (values - high.astype(F32)).astype(BF16)
    return high, low


def four(row):
    return jnp.concatenate([row, row, row, row], axis=1)


def lane_groups(table):
    wide = four(table)
    place = lax.broadcasted_iota(jnp.int32, (1, 128), 1) // WELLS
    rows = []
    for g in range(GROUPS):
        row = wide[4 * g : 4 * g + 1]
        for k in range(1, 4):
            row = jnp.where(place == k, wide[4 * g + k : 4 * g + k + 1], row)
        rows.append(row)
    return rows


def cell_parts(cell, gz):
    layer = lax.shift_right_logical(cell, 12) - gz * L
    return layer, lax.shift_right_logical(cell, 8) & (R - 1), cell & (C - 1)


def one_hot(size, target):
    return jnp.where(lax.broadcasted_iota(jnp.int32, (size, 128), 0) == target, 1.0, 0.0)


def own_rows(cell, gz):
    layer, row, _ = cell_parts(cell, gz)
    index = jnp.where(layer == -1, L + 1, layer)
    return jnp.where((layer >= -1) & (layer <= L), index * R + row, -1)


def side_rows(cell, gz, side):
    layer, row, _ = cell_parts(cell, gz)
    return jnp.where((layer >= 0) & (layer < L) & (row == (0 if side else R - 1)), layer, -1)


def shift_rows(value, by):
    return pltpu.roll(value, by % value.shape[0], 0)


def shift_columns(value, by):
    return pltpu.roll(value, by % C, 1)


def near_end(side):
    return 15 * (side % 2)


def plane(ref, side, k):
    return ref[0:L, k, :] if side < 2 else ref[k, 0:R, :]


def add_to_plane(ref, side, k, value):
    if side < 2:
        ref[0:L, k, :] += value
    else:
        ref[k, 0:R, :] += value


def set_plane(ref, side, k, value):
    if side < 2:
        ref[0:L, k, :] = value
    else:
        ref[k, 0:R, :] = value


def ends(side):
    for e in (0, 1):
        yield e, 15 * e, 2 * side + e if side < 2 else 2 * e + side - 2


def planes(ref, side, n):
    return ref[side, 16 * n : 16 * n + 16]


def inner_sum(start, p, up, down, above, below, next_row, next_col):
    value = start + next_row * shift_rows(p, -1) + shift_rows(next_row * p, 1)
    value = value + next_col * shift_columns(p, -1) + shift_columns(next_col * p, 1)
    if up is not None:
        value = value + above * up
    if down is not None:
        value = value + below * down
    return value


def sweep_layer(ref, rhs, face, l):
    return inner_sum(
        rhs[l],
        ref[l],
        ref[l + 1] if l < L - 1 else None,
        ref[l - 1] if l else None,
        face[0, l],
        face[0, l - 1] if l else None,
        face[1, l],
        face[2, l],
    )


def exchange(
    count_x,
    count_z,
    p_in,
    sat_in,
    hist_in,
    sto_in,
    vol_in,
    tr_in,
    pc_in,
    pi_in,
    ctl_in,
    tgt_in,
    storage,
    local,
    frac,
    frac_next,
    face,
    inverse,
    rhs,
    source,
    second,
    third,
    fourth,
    border,
    weight,
    over_ring,
    end_face,
    over_corner,
    bulk_in,
    bulk_out,
    mid_in,
    last_in,
    last_corner_in,
    hole,
    p0,
    total,
    trans,
    num,
    diag,
    first,
    ring,
    index_sum,
    side_index,
    own_source,
    side_source,
    own_hot,
    column_hot,
    columns_own,
    side_columns,
    near_out,
    near_in,
    corner_out,
    corner_in,
    mid_out,
    last_out,
    last_corner_out,
    perf_out,
    perf_in,
    tile_out,
    tiles,
    pc,
    pi,
    ctl,
    tgt,
    send_sem,
    recv_sem,
):
    gx, gz = lax.axis_index("gx"), lax.axis_index("gz")
    has = (gx > 0, gx < count_x - 1, gz > 0, gz < count_z - 1)

    barrier = pltpu.get_barrier_semaphore()

    def signal_column(x):
        def one(z, carry):
            pl.semaphore_signal(barrier, inc=1, device_id=(x, z), device_id_type=MESH)
            return carry

        return one

    def others(z, carry):
        @pl.when(z != gz)
        def _():
            pl.semaphore_signal(barrier, inc=1, device_id=(gx, z), device_id_type=MESH)

        return carry

    for s in (1, 0):

        @pl.when(has[s])
        def _():
            lax.fori_loop(0, count_z, signal_column(gx + 2 * s - 1), 0)

    lax.fori_loop(0, count_z, others, 0)

    loads = [
        pltpu.make_async_copy(pc_in, pc, send_sem.at[0]),
        pltpu.make_async_copy(pi_in, pi, send_sem.at[1]),
        pltpu.make_async_copy(sat_in, local.at[0], send_sem.at[2]),
        pltpu.make_async_copy(hist_in, local.at[1], send_sem.at[3]),
        pltpu.make_async_copy(p_in, p0, send_sem.at[4]),
        pltpu.make_async_copy(ctl_in, ctl, send_sem.at[5]),
        pltpu.make_async_copy(tgt_in, tgt, send_sem.at[6]),
        pltpu.make_async_copy(tr_in, trans, send_sem.at[7]),
        pltpu.make_async_copy(sto_in, storage, send_sem.at[8]),
        pltpu.make_async_copy(vol_in, local.at[2], send_sem.at[9]),
    ]
    for copy in loads:
        copy.start()

    for side in SIDES:

        @pl.when(jnp.logical_not(has[side]))
        def _():
            near_in[side] = jnp.zeros((88, C), F32)
            near_in[side, 64:80] = jnp.ones((16, C), F32)
            bulk_in[side] = jnp.zeros((48, C), F32)
            mid_in[side] = jnp.zeros((24, C), F32)
            last_in[side] = jnp.zeros((32, C), F32)
            if side < 2:
                perf_in[side] = jnp.where(
                    lax.broadcasted_iota(jnp.int32, (16, 128), 0) < GROUPS, 1e9, 0.0
                )
                tiles[8 * side : 8 * side + 4] = jnp.ones((4, 1, 128), F32)

    for c in range(4):

        @pl.when(jnp.logical_not(has[c // 2] & has[2 + c % 2]))
        def _():
            corner_in[c] = jnp.zeros((5, C), F32)
            corner_in[c, 4:5] = jnp.ones((1, C), F32)
            last_corner_in[c] = jnp.zeros((4, C), F32)

    for n in (0, 1):
        loads[n].wait()
    cell = lane_groups(pc[...])
    own_index = lane_groups(pi[...])
    own_column = [cell_parts(v, gz)[2] for v in cell]
    own_row = [own_rows(v, gz) for v in cell]
    for g in range(GROUPS):
        part = slice(128 * g, 128 * g + 128)
        own_hot[:, part] = one_hot((L + 2) * R, own_row[g]).astype(BF16)
        column_hot[:, part] = one_hot(C, own_column[g]).astype(BF16)
    for side in (0, 1):
        for g in range(GROUPS):
            perf_out[side, g : g + 1] = cell[g].astype(F32)
            perf_out[side, GROUPS + g : GROUPS + g + 1] = own_index[g]

    for n in (2, 3):
        loads[n].wait()
    for l in range(L):
        total[l], frac[l] = mobility(local[0, l], local[1, l])
    for n in (4, 7, 8):
        loads[n].wait()

    row = lax.broadcasted_iota(jnp.int32, (R, C), 0)
    column = lax.broadcasted_iota(jnp.int32, (R, C), 1)
    row_half = jnp.where(row == R - 1, 0.0, 0.5)
    column_half = jnp.where(column == C - 1, 0.0, 0.5)
    below = None
    for l in range(L):
        here = total[l]
        next_row = trans[1, l] * row_half * (here + shift_rows(here, -1))
        next_col = trans[2, l] * column_half * (here + shift_columns(here, -1))
        above = trans[0, l] * 0.5 * (here + total[l + 1]) if l < L - 1 else None
        num[l] = inner_sum(
            storage[l] * p0[l],
            p0[l],
            p0[l + 1] if l < L - 1 else None,
            p0[l - 1] if l else None,
            above,
            below,
            next_row,
            next_col,
        )
        bottom = storage[l] + next_row + shift_rows(next_row, 1)
        bottom = bottom + next_col + shift_columns(next_col, 1)
        if l:
            bottom = bottom + below
        if l < L - 1:
            bottom = bottom + above
        diag[l] = bottom
        face[0, l] = above if l < L - 1 else jnp.zeros((R, C), F32)
        face[1, l] = next_row
        face[2, l] = next_col
        below = above

    for side in SIDES:
        k = 15 - near_end(side)
        normal, along = (1, 0) if side < 2 else (0, 1)
        for n, ref in enumerate((p0, total, trans.at[normal], num, diag)):
            near_out[side, 16 * n : 16 * n + 16] = plane(ref, side, k)
        if side < 2:
            for h in (0, 1):
                perf_out[side, 8 + h : 9 + h] = trans[
                    along, L - 1, k : k + 1, 128 * h : 128 * h + 128
                ]
        else:
            near_out[side, 80:81] = trans[along, k, R - 1 : R, :]
        for n, ref in enumerate((face.at[along], face.at[2], frac)):
            bulk_out[side, 16 * n : 16 * n + 16] = plane(ref, side, k)
    for c in range(4):
        k, m = 15 - 15 * (c // 2), 15 - 15 * (c % 2)
        for n, ref in enumerate((p0, total, trans.at[0], trans.at[1], diag)):
            corner_out[c, n : n + 1] = ref[m, k : k + 1, :]

    for n in (5, 6, 9):
        loads[n].wait()
    field = total[...].reshape(L * R, C)
    parts = split(field * p0[...].reshape(L * R, C)) + split(field)
    picked = jnp.dot(
        jnp.concatenate(parts, axis=0), column_hot[...], preferred_element_type=F32
    )
    place = lax.broadcasted_iota(jnp.int32, (L * R, 128), 0)
    sums = []
    for n in (0, 1):
        part = jnp.zeros((1, 128), F32)
        for g in range(GROUPS):
            pair = picked[2 * n * L * R : 2 * (n + 1) * L * R, 128 * g : 128 * g + 128]
            chosen = jnp.where(place == own_row[g], pair[0 : L * R] + pair[L * R :], 0.0)
            part = part + own_index[g] * jnp.sum(chosen, axis=0, keepdims=True)
        part = part + pltpu.roll(part, 64, 1)
        sums.append(part + pltpu.roll(part, 32, 1))
    quarter = lax.broadcasted_iota(jnp.int32, (1, 128), 1) // WELLS
    packed = jnp.where(quarter == 0, sums[0], sums[1])
    packed = jnp.where(quarter == 2, four(tgt[...]), packed)
    packed = jnp.where(quarter == 3, four(ctl[...].astype(F32)), packed)
    tile_out[...] = packed
    tiles[4 + gz] = packed

    pl.semaphore_wait(
        barrier, count_z * (1 + has[0].astype(jnp.int32) + has[1].astype(jnp.int32)) - 1
    )

    def target(side):
        step = 1 - 2 * (side % 2)
        return (gx + step, gz) if side < 2 else (gx, gz + step)

    def remote(src, dst, send, recv, device):
        return pltpu.make_async_remote_copy(
            src_ref=src,
            dst_ref=dst,
            send_sem=send_sem.at[send],
            recv_sem=recv_sem.at[recv],
            device_id=device,
            device_id_type=MESH,
        )

    front, near, perf, bulk, mid, last = [], [], [], [], [], []
    for c in range(4):
        s, t = c // 2, 2 + c % 2
        ok = (has[s ^ 1] & has[t ^ 1], has[s] & has[t])
        to = (target(s)[0], target(t)[1])
        near.append((*ok, remote(corner_out.at[c], corner_in.at[c], 4 + c, 4 + c, to)))
        last.append((*ok, remote(last_corner_out.at[c], last_corner_in.at[c], 4 + c, 18 + c, to)))
    for side in SIDES:
        ok, to = (has[side ^ 1], has[side]), target(side)
        rows = pl.ds(0, (48, 32, 88, 88)[side])
        copy = remote(near_out.at[side, rows], near_in.at[side, rows], side, side, to)
        (front if side < 2 else near).append((*ok, copy))
        if side < 2:
            rows = pl.ds(48, 32)
            copy = remote(
                near_out.at[side, rows], near_in.at[side, rows], 13 + side, 25 + side, to
            )
            near.append((*ok, copy))
        bulk.append((*ok, remote(bulk_out.at[side], bulk_in.at[side], 15 + side, 10 + side, to)))
        mid.append((*ok, remote(mid_out.at[side], mid_in.at[side], side, 27 + side, to)))
        last.append((*ok, remote(last_out.at[side], last_in.at[side], 8 + side, 14 + side, to)))
    for side in (0, 1):
        ok, to = (has[side ^ 1], has[side]), target(side)
        perf.append((*ok, remote(perf_out.at[side], perf_in.at[side], 8 + side, 8 + side, to)))

    def start(copies):
        for out, _, copy in copies:

            @pl.when(out)
            def _():
                copy.start()

    def arrive(copies):
        for _, came, copy in copies:

            @pl.when(came)
            def _():
                copy.wait_recv()

    def sent(copies):
        for out, _, copy in copies:

            @pl.when(out)
            def _():
                copy.wait_send()

    def tile_copy(dx, z_from, z_to):
        return pltpu.make_async_remote_copy(
            src_ref=tile_out,
            dst_ref=tiles.at[4 * (1 - dx) + z_from],
            send_sem=send_sem.at[11 - dx],
            recv_sem=recv_sem.at[23 - dx],
            device_id=(gx + dx, z_to),
            device_id_type=MESH,
        )

    start(perf)
    ties = []
    for dx in (1, -1, 0):
        for z in range(4):
            if dx:
                ok = (has[1 if dx > 0 else 0], has[0 if dx > 0 else 1])
            else:
                ok = (gz != z, gz != z)
            ties.append((*ok, dx, z))
    for out, _, dx, z in ties:

        @pl.when(out)
        def _():
            tile_copy(dx, gz, z).start()

    start(front)
    start(near)


    def stacked(values):
        return jnp.concatenate(split(values), axis=0)

    def halves(values):
        n = values.shape[0] // 2
        return values[0:n] + values[n:]

    own_flat = jnp.concatenate(own_index, axis=1)
    columns_own[...] = jnp.concatenate([one_hot(C, c) for c in own_column], axis=1).T.astype(BF16)

    def own_scatter(values):
        high, low = split(values)
        rows = jnp.concatenate([own_hot[...] * high, own_hot[...] * low], axis=0)
        found = jnp.dot(rows, columns_own[...], preferred_element_type=F32)
        return halves(found).reshape(L + 2, R, C)

    index_sum[...] = own_scatter(own_flat)
    def group_wait(dx, sem):
        some = tiles.at[pl.ds(0, 4 if dx else 3)]
        pltpu.make_async_copy(some, some, sem).wait()

    def bottoms(groups):
        parts = [[tiles[4 * group + z] for z in range(4)] for group in groups]
        tile = jnp.concatenate([a + b + c + d for a, b, c, d in parts], axis=0)
        given = jnp.concatenate([group[0] for group in parts], axis=0)
        aim, mode = pltpu.roll(given, 64, 1), pltpu.roll(given, 32, 1)
        bottom = jnp.where(mode == 0.0, (aim + tile) / pltpu.roll(tile, 96, 1), aim)
        quarter = lax.broadcasted_iota(jnp.int32, bottom.shape, 1) // WELLS
        bottom = jnp.where(quarter == 0, bottom, 0.0)
        bottom = bottom + pltpu.roll(bottom, 64, 1)
        bottom = bottom + pltpu.roll(bottom, 32, 1)
        return jnp.concatenate([bottom] * GROUPS, axis=1)

    group_wait(0, recv_sem.at[23])

    bottom = bottoms([1])
    hole[...] = bottom[:, 0:WELLS]
    own_source[...] = own_scatter(own_flat * bottom)

    for l in range(L):
        src = total[l] * (own_source[l] - p0[l] * index_sum[l])
        over = 1.0 / diag[l]
        value = num[l] + src
        source[l] = src
        rhs[l] = storage[l] * p0[l] + src
        num[l] = value
        inverse[l] = over
        first[l] = value * over

    arrive(perf)
    start(bulk)

    side_rates = []
    for side in (0, 1):
        cell = [perf_in[side, g : g + 1].astype(jnp.int32) for g in range(GROUPS)]
        index = [perf_in[side, GROUPS + g : GROUPS + g + 1] for g in range(GROUPS)]
        rates = [one_hot(L, side_rows(v, gz, side)) * i for v, i in zip(cell, index)]
        side_rates.append(jnp.concatenate(rates, axis=1))
        for g in range(GROUPS):
            part = slice(128 * g, 128 * g + 128)
            side_columns[side, :, part] = one_hot(C, cell_parts(cell[g], gz)[2]).astype(BF16)

    for dx in (1, -1):

        @pl.when(has[0 if dx > 0 else 1])
        def _():
            group_wait(dx, recv_sem.at[23 - dx])

    bottom = bottoms([0, 2])
    for side in (0, 1):
        rates = side_rates[side]
        found = lax.dot_general(
            side_columns[side],
            stacked(jnp.concatenate([rates, rates * bottom[side : side + 1]], axis=0)),
            (((1,), (1,)), ((), ())),
            preferred_element_type=F32,
        )
        found = halves(found.T)
        side_index[side] = found[0:L]
        side_source[side] = found[L:]

    arrive(front)
    arrive(near[-2:])

    for side in SIDES:
        k = near_end(side)
        across = planes(near_in, side, 2)
        if side % 2:
            across = plane(trans.at[1 if side < 2 else 0], side, k)
        rate = plane(total, side, k) + planes(near_in, side, 1)
        rate = rate * across * jnp.where(has[side], 0.5, 0.0)
        border[side] = rate
        add_to_plane(diag, side, k, rate)
        add_to_plane(num, side, k, rate * planes(near_in, side, 0))

    for side in SIDES:
        k = near_end(side)
        over = 1.0 / plane(diag, side, k)
        set_plane(inverse, side, k, over)
        set_plane(first, side, k, plane(num, side, k) * over)
        weight[side] = border[side] * over

    for l in range(L):
        second[l] = sweep_layer(first, rhs, face, l) * inverse[l]

    arrive(near[:-2])

    for side in SIDES:
        k = near_end(side)
        p, here = planes(near_in, side, 0), planes(near_in, side, 1)
        if side < 2:
            well, index = side_source[side], side_index[side]
        else:
            n = L + 1 if side == 2 else L
            well, index = own_source[n], index_sum[n]
        value = planes(near_in, side, 3) + border[side] * plane(p0, side, k)
        ring[side] = value + here * (well - p * index)
        over_ring[side] = planes(near_in, side, 4) + border[side]
        for e, at, c in ends(side):
            cell = corner_in[c]
            if e and side < 2:
                rate = jnp.concatenate([perf_in[side, 8:9], perf_in[side, 9:10]], axis=1)
            elif e:
                rate = near_in[side, 80:81]
            else:
                rate = cell[2:3] if side < 2 else cell[3:4]
            rate = rate * jnp.where(has[c // 2] & has[2 + c % 2], 0.5, 0.0)
            rate = rate * (near_in[side, 16 + at : 17 + at] + cell[1:2])
            end_face[2 * side + e] = rate
            ring[side, at : at + 1] += rate * cell[0:1]
            over_ring[side, at : at + 1] += rate
        over_ring[side] = 1.0 / over_ring[side]
        add_to_plane(second, side, k, weight[side] * (ring[side] * over_ring[side]))
    for c in range(4):
        s, t = c // 2, c % 2
        over_corner[c] = 1.0 / (
            corner_in[c, 4:5] + end_face[2 * s + t] + end_face[2 * (2 + t) + s]
        )

    sent(front)
    sent(near)
    for side in SIDES:
        k = 15 - near_end(side)
        behind = 14 if k else 1
        across = plane(face.at[1 if side < 2 else 0], side, min(k, 14))
        mid_out[side, 0:16] = plane(second, side, k)
        for e in (0, 1):
            other = 2 + e if side < 2 else e
            mid_out[side, 16 + e : 17 + e] = (
                weight[other, behind : behind + 1] * across[15 * e : 15 * e + 1]
            )
    start(mid)

    for l in range(L):
        value = sweep_layer(second, rhs, face, l)
        num[l] = value
        third[l] = value * inverse[l]

    for side in SIDES:
        k = 15 - near_end(side)
        behind = 14 if k else 1
        across = plane(face.at[1 if side < 2 else 0], side, min(k, 14))
        last_out[side, 0:16] = plane(num, side, k)
        last_out[side, 16:32] = plane(rhs, side, k) + across * plane(third, side, behind)
    for c in range(4):
        k, m = 15 - 15 * (c // 2), 15 - 15 * (c % 2)
        k2, m2 = 14 if k else 1, 14 if m else 1
        last_corner_out[c, 0:1] = second[m, k : k + 1, :]
        last_corner_out[c, 1:2] = num[m, k : k + 1, :]
        last_corner_out[c, 2:3] = second[m, k2 : k2 + 1, :]
        last_corner_out[c, 3:4] = second[m2, k : k + 1, :]
    sent(perf)
    for dx in (1, -1, 0):
        out = True if dx == 0 else has[1 if dx > 0 else 0]

        @pl.when(out)
        def _():
            group_wait(dx, send_sem.at[11 - dx])

    start(last)

    for l in range(L):
        fourth[l] = sweep_layer(third, rhs, face, l) * inverse[l]

    for l in range(L):
        src, part = source[l], frac[l]
        gas_source = jnp.maximum(src, 0.0) + jnp.minimum(src, 0.0) * part
        source[l] = local[0, l] + local[2, l] * gas_source
        frac_next[0, l] = shift_rows(part, -1)
        frac_next[1, l] = shift_columns(part, -1)

    arrive(bulk)
    sent(bulk)


    arrive(mid)
    for side in SIDES:
        k = near_end(side)
        behind = 14 if k else 1
        change = weight[side] * planes(mid_in, side, 0)
        add_to_plane(third, side, k, change)
        along, col = planes(bulk_out, side ^ 1, 0), planes(bulk_out, side ^ 1, 1)
        across = plane(face.at[1 if side < 2 else 0], side, min(k, 14))
        value = inner_sum(jnp.zeros((16, C), F32), change, None, None, None, None, along, col)
        add_to_plane(fourth, side, k, value * plane(inverse, side, k))
        add_to_plane(fourth, side, behind, across * change * plane(inverse, side, behind))
    sent(mid)

    arrive(last)
    sent(last)


def solve(
    storage,
    local,
    frac,
    frac_next,
    face,
    inverse,
    rhs,
    source,
    second,
    third,
    fourth,
    border,
    weight,
    over_ring,
    end_face,
    over_corner,
    bulk_in,
    bulk_out,
    mid_in,
    last_in,
    last_corner_in,
    hole,
    new_p,
    residual,
    new_s,
    new_h,
    new_hole,
    flows,
    out_r,
    out_s,
    out_h,
    sems,
):
    writes = [pltpu.make_async_copy(hole, new_hole, sems.at[1, 3])]
    writes[0].start()
    spot = lax.broadcasted_iota(jnp.int32, (16, C), 0)
    corners = []
    for c in range(4):
        s, t = c // 2, c % 2
        value = last_corner_in[c, 1:2]
        value = value + end_face[2 * s + t] * mid_in[s, 15 * t : 15 * t + 1]
        value = value + end_face[2 * (2 + t) + s] * mid_in[2 + t, 15 * s : 15 * s + 1]
        corners.append(value * over_corner[c])
    rings, parts = [], []
    for side in SIDES:
        k = near_end(side)
        rate = border[side]
        value = planes(last_in, side, 0) + rate * plane(second, side, k)
        add = planes(last_in, side, 1)
        for e, at, c in ends(side):
            cell = last_corner_in[c]
            value = value + jnp.where(spot == at, end_face[2 * side + e] * cell[0:1], 0.0)
            far = cell[2:3] if side < 2 else cell[3:4]
            add = add + jnp.where(spot == at, mid_in[side, 16 + e : 17 + e] * far, 0.0)
            add = add + jnp.where(spot == at, end_face[2 * side + e] * corners[c], 0.0)
        value = value * over_ring[side]
        rings.append(value)
        along, col = planes(bulk_in, side, 0), planes(bulk_in, side, 1)
        parts.append(inner_sum(add, value, None, None, None, None, along, col))
    for side in SIDES:
        add_to_plane(fourth, side, near_end(side), weight[side] * rings[side])

    writes.append(pltpu.make_async_copy(fourth, new_p, sems.at[0, 3]))
    writes[1].start()
    for side in SIDES:
        k = near_end(side)
        outer = (parts[side] + border[side] * plane(third, side, k)) * over_ring[side]
        rate = -border[side] if side == 0 else border[side]
        flow = rate * (plane(fourth, side, k) - outer)
        flows[side, 0] = flow
        flows[side, 1] = flow * jnp.where(
            (flow < 0) if side == 0 else (flow > 0),
            planes(bulk_out, side ^ 1, 2),
            planes(bulk_in, side, 2),
        )

    first_row, last_row = spot == 0, spot == R - 1
    below = gas_below = None
    for l in range(L):
        p, part = fourth[l], frac[l]
        flow = face[1, l] * (p - shift_rows(p, -1))
        gas = flow * jnp.where(flow > 0, part, frac_next[0, l])
        flow = jnp.where(last_row, flows[1, 0, l : l + 1], flow)
        gas = jnp.where(last_row, flows[1, 1, l : l + 1], gas)
        net = flow - jnp.where(first_row, flows[0, 0, l : l + 1], shift_rows(flow, 1))
        out = gas - jnp.where(first_row, flows[0, 1, l : l + 1], shift_rows(gas, 1))
        flow = face[2, l] * (p - shift_columns(p, -1))
        gas = flow * jnp.where(flow > 0, part, frac_next[1, l])
        net = net + flow - shift_columns(flow, 1)
        out = out + gas - shift_columns(gas, 1)
        if l:
            net, out = net - below, out - gas_below
        else:
            net, out = net + flows[2, 0], out + flows[2, 1]
        if l < L - 1:
            below = face[0, l] * (p - fourth[l + 1])
            gas_below = below * jnp.where(below > 0, part, frac[l + 1])
        else:
            below, gas_below = flows[3, 0], flows[3, 1]
        net, out = net + below, out + gas_below
        out_r[l] = rhs[l] - storage[l] * p - net
        saturation = source[l] - local[2, l] * out
        out_s[l] = saturation
        out_h[l] = jnp.maximum(local[1, l], saturation)
        if l % 8 == 7:
            part = pl.ds(l - 7, 8)
            for n, (src, dst) in enumerate(
                ((out_r, residual), (out_s, new_s), (out_h, new_h))
            ):
                copy = pltpu.make_async_copy(src.at[part], dst.at[part], sems.at[l // 8, n])
                copy.start()
                writes.append(copy)
    for copy in writes:
        copy.wait()


def body(
    count_x,
    count_z,
    pressure,
    saturation,
    sat_history,
    storage,
    step_volume,
    transmiss,
    perf_cell,
    perf_index,
    control,
    target,
):
    vmem = pl.BlockSpec(memory_space=pltpu.VMEM)
    hbm = pl.BlockSpec(memory_space=pltpu.HBM)
    dma = pltpu.SemaphoreType.DMA
    block = (L, R, C)
    side = (4, 16, C)
    mid = pl.pallas_call(
        functools.partial(exchange, count_x, count_z),
        out_shape=[
            pltpu.VMEM(shape, F32)
            for shape in (
                block,
                (3, *block),
                block,
                (2, *block),
                (3, *block),
                *[block] * 6,
                *[side] * 3,
                (8, 1, C),
                (4, 1, C),
                *[(4, 48, C)] * 2,
                (4, 24, C),
                (4, 32, C),
                (4, 4, C),
                (1, WELLS),
            )
        ],
        in_specs=[hbm] * 10,
        out_specs=[vmem] * 22,
        scratch_shapes=[
            pltpu.VMEM(block, F32),
            pltpu.VMEM(block, F32),
            pltpu.VMEM((3, *block), F32),
            *[pltpu.VMEM(block, F32)] * 3,
            pltpu.VMEM(side, F32),
            pltpu.VMEM((L + 2, R, C), F32),
            pltpu.VMEM((2, L, C), F32),
            pltpu.VMEM((L + 2, R, C), F32),
            pltpu.VMEM((2, L, C), F32),
            pltpu.VMEM(((L + 2) * R, 512), BF16),
            pltpu.VMEM((C, 512), BF16),
            pltpu.VMEM((512, C), BF16),
            pltpu.VMEM((2, C, 512), BF16),
            *[pltpu.VMEM((4, 88, C), F32)] * 2,
            *[pltpu.VMEM((4, 5, C), F32)] * 2,
            pltpu.VMEM((4, 24, C), F32),
            pltpu.VMEM((4, 32, C), F32),
            pltpu.VMEM((4, 4, C), F32),
            *[pltpu.VMEM((2, 16, 128), F32)] * 2,
            pltpu.VMEM((1, 128), F32),
            pltpu.VMEM((12, 1, 128), F32),
            pltpu.VMEM((NP, WELLS), jnp.int32),
            pltpu.VMEM((NP, WELLS), F32),
            pltpu.VMEM((1, WELLS), jnp.int32),
            pltpu.VMEM((1, WELLS), F32),
            dma((19,)),
            dma((31,)),
        ],
        compiler_params=pltpu.CompilerParams(
            collective_id=0, has_side_effects=True, vmem_limit_bytes=VMEM_LIMIT
        ),
        name="exchange",
    )(
        *[
            pltpu.with_memory_space_constraint(values, pltpu.HBM)
            for values in (
                pressure,
                saturation,
                sat_history,
                storage,
                step_volume,
                transmiss,
                perf_cell.T,
                perf_index.T,
                control.reshape(1, WELLS),
                target.reshape(1, WELLS),
            )
        ]
    )
    *fields, hole = pl.pallas_call(
        solve,
        out_shape=[jax.ShapeDtypeStruct(block, F32)] * 4
        + [jax.ShapeDtypeStruct((1, WELLS), F32)],
        in_specs=[vmem] * 22,
        out_specs=[hbm] * 5,
        scratch_shapes=[
            pltpu.VMEM((4, 2, 16, C), F32),
            *[pltpu.VMEM(block, F32)] * 3,
            dma((2, 4)),
        ],
        compiler_params=pltpu.CompilerParams(vmem_limit_bytes=VMEM_LIMIT),
        name="solve",
    )(*mid)
    return (*fields, hole.reshape(WELLS))


def solution(mesh):
    cells = P("gz", "gx", None)
    return jax.shard_map(
        functools.partial(body, mesh.shape["gx"], mesh.shape["gz"]),
        mesh=mesh,
        in_specs=(
            *[cells] * 5,
            P(None, "gz", "gx", None),
            P("gx", None),
            P("gx", None),
            P("gx"),
            P("gx"),
        ),
        out_specs=(*[cells] * 4, P("gx")),
        check_vma=False,
    )
```

```python
import functools

import jax
import jax.numpy as jnp
from jax import lax
from jax.experimental import pallas as pl
from jax.experimental.pallas import tpu as pltpu
from jax.sharding import PartitionSpec as P

L = 16
R = 16
C = 256
WELLS = 32
NP = 16
GROUPS = WELLS * NP // 128
SIDES = range(4)
MESH = pl.DeviceIdType.MESH
F32 = jnp.float32
BF16 = jnp.bfloat16
VMEM_LIMIT = 26 * 2**20


def mobility(sat, history):
    trapped = history / (1.0 + 1.5 * history)
    excess = jnp.maximum(sat - trapped, 0.0)
    free_gas = 0.5 * (excess + jnp.sqrt(excess * excess + excess / 0.375))
    relperm = jnp.where(sat < history, free_gas * free_gas, sat * sat)
    gas = relperm / 0.5
    total = (1.0 - sat) * (1.0 - sat) + gas
    return (total, gas / total)


def split(values):
    high = values.astype(BF16)
    low = (values - high.astype(F32)).astype(BF16)
    return high, low


def four(row):
    return jnp.concatenate([row, row, row, row], axis=1)


def lane_groups(table):
    wide = four(table)
    place = lax.broadcasted_iota(jnp.int32, (1, 128), 1) // WELLS
    rows = []
    for g in range(GROUPS):
        row = wide[4 * g : 4 * g + 1]
        for k in range(1, 4):
            row = jnp.where(place == k, wide[4 * g + k : 4 * g + k + 1], row)
        rows.append(row)
    return rows


def cell_parts(cell, gz):
    layer = lax.shift_right_logical(cell, 12) - gz * L
    return layer, lax.shift_right_logical(cell, 8) & (R - 1), cell & (C - 1)


def one_hot(size, target):
    return jnp.where(lax.broadcasted_iota(jnp.int32, (size, 128), 0) == target, 1.0, 0.0)


def own_rows(cell, gz):
    layer, row, _ = cell_parts(cell, gz)
    index = jnp.where(layer == -1, L + 1, layer)
    return jnp.where((layer >= -1) & (layer <= L), index * R + row, -1)


def side_rows(cell, gz, side):
    layer, row, _ = cell_parts(cell, gz)
    return jnp.where((layer >= 0) & (layer < L) & (row == (0 if side else R - 1)), layer, -1)


def shift_rows(value, by):
    return pltpu.roll(value, by % value.shape[0], 0)


def shift_columns(value, by):
    return pltpu.roll(value, by % C, 1)


def near_end(side):
    return 15 * (side % 2)


def plane(ref, side, k):
    return ref[0:L, k, :] if side < 2 else ref[k, 0:R, :]


def add_to_plane(ref, side, k, value):
    if side < 2:
        ref[0:L, k, :] += value
    else:
        ref[k, 0:R, :] += value


def set_plane(ref, side, k, value):
    if side < 2:
        ref[0:L, k, :] = value
    else:
        ref[k, 0:R, :] = value


def ends(side):
    for e in (0, 1):
        yield e, 15 * e, 2 * side + e if side < 2 else 2 * e + side - 2


def planes(ref, side, n):
    return ref[side, 16 * n : 16 * n + 16]


def inner_sum(start, p, up, down, above, below, next_row, next_col):
    value = start + next_row * shift_rows(p, -1) + shift_rows(next_row * p, 1)
    value = value + next_col * shift_columns(p, -1) + shift_columns(next_col * p, 1)
    if up is not None:
        value = value + above * up
    if down is not None:
        value = value + below * down
    return value


def sweep_layer(ref, rhs, face, l):
    return inner_sum(
        rhs[l],
        ref[l],
        ref[l + 1] if l < L - 1 else None,
        ref[l - 1] if l else None,
        face[0, l],
        face[0, l - 1] if l else None,
        face[1, l],
        face[2, l],
    )


def exchange(
    count_x,
    count_z,
    p_in,
    sat_in,
    hist_in,
    sto_in,
    vol_in,
    tr_in,
    pc_in,
    pi_in,
    ctl_in,
    tgt_in,
    storage,
    local,
    frac,
    frac_next,
    face,
    inverse,
    rhs,
    source,
    second,
    third,
    fourth,
    border,
    weight,
    over_ring,
    end_face,
    over_corner,
    bulk_in,
    bulk_out,
    mid_in,
    last_in,
    last_corner_in,
    hole,
    p0,
    total,
    trans,
    num,
    diag,
    first,
    ring,
    index_sum,
    side_index,
    own_source,
    side_source,
    own_hot,
    column_hot,
    columns_own,
    side_columns,
    near_out,
    near_in,
    corner_out,
    corner_in,
    mid_out,
    last_out,
    last_corner_out,
    perf_out,
    perf_in,
    tile_out,
    tiles,
    pc,
    pi,
    ctl,
    tgt,
    send_sem,
    recv_sem,
):
    gx, gz = lax.axis_index("gx"), lax.axis_index("gz")
    has = (gx > 0, gx < count_x - 1, gz > 0, gz < count_z - 1)

    barrier = pltpu.get_barrier_semaphore()

    def signal_column(x):
        def one(z, carry):
            pl.semaphore_signal(barrier, inc=1, device_id=(x, z), device_id_type=MESH)
            return carry

        return one

    def others(z, carry):
        @pl.when(z != gz)
        def _():
            pl.semaphore_signal(barrier, inc=1, device_id=(gx, z), device_id_type=MESH)

        return carry

    for s in (1, 0):

        @pl.when(has[s])
        def _():
            lax.fori_loop(0, count_z, signal_column(gx + 2 * s - 1), 0)

    lax.fori_loop(0, count_z, others, 0)

    loads = [
        pltpu.make_async_copy(pc_in, pc, send_sem.at[0]),
        pltpu.make_async_copy(pi_in, pi, send_sem.at[1]),
        pltpu.make_async_copy(sat_in, local.at[0], send_sem.at[2]),
        pltpu.make_async_copy(hist_in, local.at[1], send_sem.at[3]),
        pltpu.make_async_copy(p_in, p0, send_sem.at[4]),
        pltpu.make_async_copy(ctl_in, ctl, send_sem.at[5]),
        pltpu.make_async_copy(tgt_in, tgt, send_sem.at[6]),
        pltpu.make_async_copy(tr_in, trans, send_sem.at[7]),
        pltpu.make_async_copy(sto_in, storage, send_sem.at[8]),
        pltpu.make_async_copy(vol_in, local.at[2], send_sem.at[9]),
    ]
    for copy in loads:
        copy.start()

    for side in SIDES:

        @pl.when(jnp.logical_not(has[side]))
        def _():
            near_in[side] = jnp.zeros((88, C), F32)
            near_in[side, 64:80] = jnp.ones((16, C), F32)
            bulk_in[side] = jnp.zeros((48, C), F32)
            mid_in[side] = jnp.zeros((24, C), F32)
            last_in[side] = jnp.zeros((32, C), F32)
            if side < 2:
                perf_in[side] = jnp.where(
                    lax.broadcasted_iota(jnp.int32, (16, 128), 0) < GROUPS, 1e9, 0.0
                )
                tiles[8 * side : 8 * side + 4] = jnp.ones((4, 1, 128), F32)

    for c in range(4):

        @pl.when(jnp.logical_not(has[c // 2] & has[2 + c % 2]))
        def _():
            corner_in[c] = jnp.zeros((5, C), F32)
            corner_in[c, 4:5] = jnp.ones((1, C), F32)
            last_corner_in[c] = jnp.zeros((4, C), F32)

    for n in (0, 1):
        loads[n].wait()
    cell = lane_groups(pc[...])
    own_index = lane_groups(pi[...])
    own_column = [cell_parts(v, gz)[2] for v in cell]
    own_row = [own_rows(v, gz) for v in cell]
    for g in range(GROUPS):
        part = slice(128 * g, 128 * g + 128)
        own_hot[:, part] = one_hot((L + 2) * R, own_row[g]).astype(BF16)
        column_hot[:, part] = one_hot(C, own_column[g]).astype(BF16)
    for side in (0, 1):
        for g in range(GROUPS):
            perf_out[side, g : g + 1] = cell[g].astype(F32)
            perf_out[side, GROUPS + g : GROUPS + g + 1] = own_index[g]

    for n in (2, 3):
        loads[n].wait()
    for l in range(L):
        total[l], frac[l] = mobility(local[0, l], local[1, l])
    for n in (4, 7, 8):
        loads[n].wait()

    row = lax.broadcasted_iota(jnp.int32, (R, C), 0)
    column = lax.broadcasted_iota(jnp.int32, (R, C), 1)
    row_half = jnp.where(row == R - 1, 0.0, 0.5)
    column_half = jnp.where(column == C - 1, 0.0, 0.5)
    below = None
    for l in range(L):
        here = total[l]
        next_row = trans[1, l] * row_half * (here + shift_rows(here, -1))
        next_col = trans[2, l] * column_half * (here + shift_columns(here, -1))
        above = trans[0, l] * 0.5 * (here + total[l + 1]) if l < L - 1 else None
        num[l] = inner_sum(
            storage[l] * p0[l],
            p0[l],
            p0[l + 1] if l < L - 1 else None,
            p0[l - 1] if l else None,
            above,
            below,
            next_row,
            next_col,
        )
        bottom = storage[l] + next_row + shift_rows(next_row, 1)
        bottom = bottom + next_col + shift_columns(next_col, 1)
        if l:
            bottom = bottom + below
        if l < L - 1:
            bottom = bottom + above
        diag[l] = bottom
        face[0, l] = above if l < L - 1 else jnp.zeros((R, C), F32)
        face[1, l] = next_row
        face[2, l] = next_col
        below = above

    for side in SIDES:
        k = 15 - near_end(side)
        normal, along = (1, 0) if side < 2 else (0, 1)
        for n, ref in enumerate((p0, total, trans.at[normal], num, diag)):
            near_out[side, 16 * n : 16 * n + 16] = plane(ref, side, k)
        if side < 2:
            for h in (0, 1):
                perf_out[side, 8 + h : 9 + h] = trans[
                    along, L - 1, k : k + 1, 128 * h : 128 * h + 128
                ]
        else:
            near_out[side, 80:81] = trans[along, k, R - 1 : R, :]
        for n, ref in enumerate((face.at[along], face.at[2], frac)):
            bulk_out[side, 16 * n : 16 * n + 16] = plane(ref, side, k)
    for c in range(4):
        k, m = 15 - 15 * (c // 2), 15 - 15 * (c % 2)
        for n, ref in enumerate((p0, total, trans.at[0], trans.at[1], diag)):
            corner_out[c, n : n + 1] = ref[m, k : k + 1, :]

    for n in (5, 6, 9):
        loads[n].wait()
    field = total[...].reshape(L * R, C)
    parts = split(field * p0[...].reshape(L * R, C)) + split(field)
    picked = jnp.dot(
        jnp.concatenate(parts, axis=0), column_hot[...], preferred_element_type=F32
    )
    place = lax.broadcasted_iota(jnp.int32, (L * R, 128), 0)
    sums = []
    for n in (0, 1):
        part = jnp.zeros((1, 128), F32)
        for g in range(GROUPS):
            pair = picked[2 * n * L * R : 2 * (n + 1) * L * R, 128 * g : 128 * g + 128]
            chosen = jnp.where(place == own_row[g], pair[0 : L * R] + pair[L * R :], 0.0)
            part = part + own_index[g] * jnp.sum(chosen, axis=0, keepdims=True)
        part = part + pltpu.roll(part, 64, 1)
        sums.append(part + pltpu.roll(part, 32, 1))
    quarter = lax.broadcasted_iota(jnp.int32, (1, 128), 1) // WELLS
    packed = jnp.where(quarter == 0, sums[0], sums[1])
    packed = jnp.where(quarter == 2, four(tgt[...]), packed)
    packed = jnp.where(quarter == 3, four(ctl[...].astype(F32)), packed)
    tile_out[...] = packed
    tiles[4 + gz] = packed

    pl.semaphore_wait(
        barrier, count_z * (1 + has[0].astype(jnp.int32) + has[1].astype(jnp.int32)) - 1
    )

    def target(side):
        step = 1 - 2 * (side % 2)
        return (gx + step, gz) if side < 2 else (gx, gz + step)

    def remote(src, dst, send, recv, device):
        return pltpu.make_async_remote_copy(
            src_ref=src,
            dst_ref=dst,
            send_sem=send_sem.at[send],
            recv_sem=recv_sem.at[recv],
            device_id=device,
            device_id_type=MESH,
        )

    front, near, perf, bulk, mid, last = [], [], [], [], [], []
    for c in range(4):
        s, t = c // 2, 2 + c % 2
        ok = (has[s ^ 1] & has[t ^ 1], has[s] & has[t])
        to = (target(s)[0], target(t)[1])
        near.append((*ok, remote(corner_out.at[c], corner_in.at[c], 4 + c, 4 + c, to)))
        last.append((*ok, remote(last_corner_out.at[c], last_corner_in.at[c], 4 + c, 18 + c, to)))
    for side in SIDES:
        ok, to = (has[side ^ 1], has[side]), target(side)
        rows = pl.ds(0, (48, 32, 88, 88)[side])
        copy = remote(near_out.at[side, rows], near_in.at[side, rows], side, side, to)
        (front if side < 2 else near).append((*ok, copy))
        if side < 2:
            rows = pl.ds(48, 32)
            copy = remote(
                near_out.at[side, rows], near_in.at[side, rows], 13 + side, 25 + side, to
            )
            near.append((*ok, copy))
        bulk.append((*ok, remote(bulk_out.at[side], bulk_in.at[side], 15 + side, 10 + side, to)))
        mid.append((*ok, remote(mid_out.at[side], mid_in.at[side], side, 27 + side, to)))
        last.append((*ok, remote(last_out.at[side], last_in.at[side], 8 + side, 14 + side, to)))
    for side in (0, 1):
        ok, to = (has[side ^ 1], has[side]), target(side)
        perf.append((*ok, remote(perf_out.at[side], perf_in.at[side], 8 + side, 8 + side, to)))

    def start(copies):
        for out, _, copy in copies:

            @pl.when(out)
            def _():
                copy.start()

    def arrive(copies):
        for _, came, copy in copies:

            @pl.when(came)
            def _():
                copy.wait_recv()

    def sent(copies):
        for out, _, copy in copies:

            @pl.when(out)
            def _():
                copy.wait_send()

    def tile_copy(dx, z_from, z_to):
        return pltpu.make_async_remote_copy(
            src_ref=tile_out,
            dst_ref=tiles.at[4 * (1 - dx) + z_from],
            send_sem=send_sem.at[11 - dx],
            recv_sem=recv_sem.at[23 - dx],
            device_id=(gx + dx, z_to),
            device_id_type=MESH,
        )

    start(perf)
    ties = []
    for dx in (1, -1, 0):
        for z in range(4):
            if dx:
                ok = (has[1 if dx > 0 else 0], has[0 if dx > 0 else 1])
            else:
                ok = (gz != z, gz != z)
            ties.append((*ok, dx, z))
    for out, _, dx, z in ties:

        @pl.when(out)
        def _():
            tile_copy(dx, gz, z).start()

    start(front)
    start(near)


    def stacked(values):
        return jnp.concatenate(split(values), axis=0)

    def halves(values):
        n = values.shape[0] // 2
        return values[0:n] + values[n:]

    own_flat = jnp.concatenate(own_index, axis=1)
    columns_own[...] = jnp.concatenate([one_hot(C, c) for c in own_column], axis=1).T.astype(BF16)

    def own_scatter(values):
        high, low = split(values)
        rows = jnp.concatenate([own_hot[...] * high, own_hot[...] * low], axis=0)
        found = jnp.dot(rows, columns_own[...], preferred_element_type=F32)
        return halves(found).reshape(L + 2, R, C)

    index_sum[...] = own_scatter(own_flat)
    def group_wait(dx, sem):
        some = tiles.at[pl.ds(0, 4 if dx else 3)]
        pltpu.make_async_copy(some, some, sem).wait()

    def bottoms(groups):
        parts = [[tiles[4 * group + z] for z in range(4)] for group in groups]
        tile = jnp.concatenate([a + b + c + d for a, b, c, d in parts], axis=0)
        given = jnp.concatenate([group[0] for group in parts], axis=0)
        aim, mode = pltpu.roll(given, 64, 1), pltpu.roll(given, 32, 1)
        bottom = jnp.where(mode == 0.0, (aim + tile) / pltpu.roll(tile, 96, 1), aim)
        quarter = lax.broadcasted_iota(jnp.int32, bottom.shape, 1) // WELLS
        bottom = jnp.where(quarter == 0, bottom, 0.0)
        bottom = bottom + pltpu.roll(bottom, 64, 1)
        bottom = bottom + pltpu.roll(bottom, 32, 1)
        return jnp.concatenate([bottom] * GROUPS, axis=1)

    group_wait(0, recv_sem.at[23])

    bottom = bottoms([1])
    hole[...] = bottom[:, 0:WELLS]
    own_source[...] = own_scatter(own_flat * bottom)

    for l in range(L):
        src = total[l] * (own_source[l] - p0[l] * index_sum[l])
        over = 1.0 / diag[l]
        value = num[l] + src
        source[l] = src
        rhs[l] = storage[l] * p0[l] + src
        num[l] = value
        inverse[l] = over
        first[l] = value * over

    arrive(perf)
    start(bulk)

    side_rates = []
    for side in (0, 1):
        cell = [perf_in[side, g : g + 1].astype(jnp.int32) for g in range(GROUPS)]
        index = [perf_in[side, GROUPS + g : GROUPS + g + 1] for g in range(GROUPS)]
        rates = [one_hot(L, side_rows(v, gz, side)) * i for v, i in zip(cell, index)]
        side_rates.append(jnp.concatenate(rates, axis=1))
        for g in range(GROUPS):
            part = slice(128 * g, 128 * g + 128)
            side_columns[side, :, part] = one_hot(C, cell_parts(cell[g], gz)[2]).astype(BF16)

    for dx in (1, -1):

        @pl.when(has[0 if dx > 0 else 1])
        def _():
            group_wait(dx, recv_sem.at[23 - dx])

    bottom = bottoms([0, 2])
    for side in (0, 1):
        rates = side_rates[side]
        found = lax.dot_general(
            side_columns[side],
            stacked(jnp.concatenate([rates, rates * bottom[side : side + 1]], axis=0)),
            (((1,), (1,)), ((), ())),
            preferred_element_type=F32,
        )
        found = halves(found.T)
        side_index[side] = found[0:L]
        side_source[side] = found[L:]

    arrive(front)
    arrive(near[-2:])

    for side in SIDES:
        k = near_end(side)
        across = planes(near_in, side, 2)
        if side % 2:
            across = plane(trans.at[1 if side < 2 else 0], side, k)
        rate = plane(total, side, k) + planes(near_in, side, 1)
        rate = rate * across * jnp.where(has[side], 0.5, 0.0)
        border[side] = rate
        add_to_plane(diag, side, k, rate)
        add_to_plane(num, side, k, rate * planes(near_in, side, 0))

    for side in SIDES:
        k = near_end(side)
        over = 1.0 / plane(diag, side, k)
        set_plane(inverse, side, k, over)
        set_plane(first, side, k, plane(num, side, k) * over)
        weight[side] = border[side] * over

    for l in range(L):
        second[l] = sweep_layer(first, rhs, face, l) * inverse[l]

    arrive(near[:-2])

    for side in SIDES:
        k = near_end(side)
        p, here = planes(near_in, side, 0), planes(near_in, side, 1)
        if side < 2:
            well, index = side_source[side], side_index[side]
        else:
            n = L + 1 if side == 2 else L
            well, index = own_source[n], index_sum[n]
        value = planes(near_in, side, 3) + border[side] * plane(p0, side, k)
        ring[side] = value + here * (well - p * index)
        over_ring[side] = planes(near_in, side, 4) + border[side]
        for e, at, c in ends(side):
            cell = corner_in[c]
            if e and side < 2:
                rate = jnp.concatenate([perf_in[side, 8:9], perf_in[side, 9:10]], axis=1)
            elif e:
                rate = near_in[side, 80:81]
            else:
                rate = cell[2:3] if side < 2 else cell[3:4]
            rate = rate * jnp.where(has[c // 2] & has[2 + c % 2], 0.5, 0.0)
            rate = rate * (near_in[side, 16 + at : 17 + at] + cell[1:2])
            end_face[2 * side + e] = rate
            ring[side, at : at + 1] += rate * cell[0:1]
            over_ring[side, at : at + 1] += rate
        over_ring[side] = 1.0 / over_ring[side]
        add_to_plane(second, side, k, weight[side] * (ring[side] * over_ring[side]))
    for c in range(4):
        s, t = c // 2, c % 2
        over_corner[c] = 1.0 / (
            corner_in[c, 4:5] + end_face[2 * s + t] + end_face[2 * (2 + t) + s]
        )

    sent(front)
    sent(near)
    for side in SIDES:
        k = 15 - near_end(side)
        behind = 14 if k else 1
        across = plane(face.at[1 if side < 2 else 0], side, min(k, 14))
        mid_out[side, 0:16] = plane(second, side, k)
        for e in (0, 1):
            other = 2 + e if side < 2 else e
            mid_out[side, 16 + e : 17 + e] = (
                weight[other, behind : behind + 1] * across[15 * e : 15 * e + 1]
            )
    start(mid)

    for l in range(L):
        value = sweep_layer(second, rhs, face, l)
        num[l] = value
        third[l] = value * inverse[l]

    for side in SIDES:
        k = 15 - near_end(side)
        behind = 14 if k else 1
        across = plane(face.at[1 if side < 2 else 0], side, min(k, 14))
        last_out[side, 0:16] = plane(num, side, k)
        last_out[side, 16:32] = plane(rhs, side, k) + across * plane(third, side, behind)
    for c in range(4):
        k, m = 15 - 15 * (c // 2), 15 - 15 * (c % 2)
        k2, m2 = 14 if k else 1, 14 if m else 1
        last_corner_out[c, 0:1] = second[m, k : k + 1, :]
        last_corner_out[c, 1:2] = num[m, k : k + 1, :]
        last_corner_out[c, 2:3] = second[m, k2 : k2 + 1, :]
        last_corner_out[c, 3:4] = second[m2, k : k + 1, :]
    sent(perf)
    for dx in (1, -1, 0):
        out = True if dx == 0 else has[1 if dx > 0 else 0]

        @pl.when(out)
        def _():
            group_wait(dx, send_sem.at[11 - dx])

    start(last)

    for l in range(L):
        fourth[l] = sweep_layer(third, rhs, face, l) * inverse[l]

    for l in range(L):
        src, part = source[l], frac[l]
        gas_source = jnp.maximum(src, 0.0) + jnp.minimum(src, 0.0) * part
        source[l] = local[0, l] + local[2, l] * gas_source
        frac_next[0, l] = shift_rows(part, -1)
        frac_next[1, l] = shift_columns(part, -1)

    arrive(bulk)
    sent(bulk)


    arrive(mid)
    for side in SIDES:
        k = near_end(side)
        behind = 14 if k else 1
        change = weight[side] * planes(mid_in, side, 0)
        add_to_plane(third, side, k, change)
        along, col = planes(bulk_out, side ^ 1, 0), planes(bulk_out, side ^ 1, 1)
        across = plane(face.at[1 if side < 2 else 0], side, min(k, 14))
        value = inner_sum(jnp.zeros((16, C), F32), change, None, None, None, None, along, col)
        add_to_plane(fourth, side, k, value * plane(inverse, side, k))
        add_to_plane(fourth, side, behind, across * change * plane(inverse, side, behind))
    sent(mid)

    arrive(last)
    sent(last)


def solve(
    storage,
    local,
    frac,
    frac_next,
    face,
    inverse,
    rhs,
    source,
    second,
    third,
    fourth,
    border,
    weight,
    over_ring,
    end_face,
    over_corner,
    bulk_in,
    bulk_out,
    mid_in,
    last_in,
    last_corner_in,
    hole,
    new_p,
    residual,
    new_s,
    new_h,
    new_hole,
    flows,
    out_r,
    out_s,
    out_h,
    sems,
):
    writes = [pltpu.make_async_copy(hole, new_hole, sems.at[1, 3])]
    writes[0].start()
    spot = lax.broadcasted_iota(jnp.int32, (16, C), 0)
    corners = []
    for c in range(4):
        s, t = c // 2, c % 2
        value = last_corner_in[c, 1:2]
        value = value + end_face[2 * s + t] * mid_in[s, 15 * t : 15 * t + 1]
        value = value + end_face[2 * (2 + t) + s] * mid_in[2 + t, 15 * s : 15 * s + 1]
        corners.append(value * over_corner[c])
    rings, parts = [], []
    for side in SIDES:
        k = near_end(side)
        rate = border[side]
        value = planes(last_in, side, 0) + rate * plane(second, side, k)
        add = planes(last_in, side, 1)
        for e, at, c in ends(side):
            cell = last_corner_in[c]
            value = value + jnp.where(spot == at, end_face[2 * side + e] * cell[0:1], 0.0)
            far = cell[2:3] if side < 2 else cell[3:4]
            add = add + jnp.where(spot == at, mid_in[side, 16 + e : 17 + e] * far, 0.0)
            add = add + jnp.where(spot == at, end_face[2 * side + e] * corners[c], 0.0)
        value = value * over_ring[side]
        rings.append(value)
        along, col = planes(bulk_in, side, 0), planes(bulk_in, side, 1)
        parts.append(inner_sum(add, value, None, None, None, None, along, col))
    for side in SIDES:
        add_to_plane(fourth, side, near_end(side), weight[side] * rings[side])

    writes.append(pltpu.make_async_copy(fourth, new_p, sems.at[0, 3]))
    writes[1].start()
    for side in SIDES:
        k = near_end(side)
        outer = (parts[side] + border[side] * plane(third, side, k)) * over_ring[side]
        rate = -border[side] if side == 0 else border[side]
        flow = rate * (plane(fourth, side, k) - outer)
        flows[side, 0] = flow
        flows[side, 1] = flow * jnp.where(
            (flow < 0) if side == 0 else (flow > 0),
            planes(bulk_out, side ^ 1, 2),
            planes(bulk_in, side, 2),
        )

    first_row, last_row = spot == 0, spot == R - 1
    below = gas_below = None
    for l in range(L):
        p, part = fourth[l], frac[l]
        flow = face[1, l] * (p - shift_rows(p, -1))
        gas = flow * jnp.where(flow > 0, part, frac_next[0, l])
        flow = jnp.where(last_row, flows[1, 0, l : l + 1], flow)
        gas = jnp.where(last_row, flows[1, 1, l : l + 1], gas)
        net = flow - jnp.where(first_row, flows[0, 0, l : l + 1], shift_rows(flow, 1))
        out = gas - jnp.where(first_row, flows[0, 1, l : l + 1], shift_rows(gas, 1))
        flow = face[2, l] * (p - shift_columns(p, -1))
        gas = flow * jnp.where(flow > 0, part, frac_next[1, l])
        net = net + flow - shift_columns(flow, 1)
        out = out + gas - shift_columns(gas, 1)
        if l:
            net, out = net - below, out - gas_below
        else:
            net, out = net + flows[2, 0], out + flows[2, 1]
        if l < L - 1:
            below = face[0, l] * (p - fourth[l + 1])
            gas_below = below * jnp.where(below > 0, part, frac[l + 1])
        else:
            below, gas_below = flows[3, 0], flows[3, 1]
        net, out = net + below, out + gas_below
        out_r[l] = rhs[l] - storage[l] * p - net
        saturation = source[l] - local[2, l] * out
        out_s[l] = saturation
        out_h[l] = jnp.maximum(local[1, l], saturation)
        if l in (7, 12, 15):
            chunk = (7, 12, 15).index(l)
            part = (pl.ds(0, 8), pl.ds(8, 5), pl.ds(13, 3))[chunk]
            for n, (src, dst) in enumerate(
                ((out_r, residual), (out_s, new_s), (out_h, new_h))
            ):
                copy = pltpu.make_async_copy(src.at[part], dst.at[part], sems.at[chunk, n])
                copy.start()
                writes.append(copy)
    for copy in writes:
        copy.wait()


def body(
    count_x,
    count_z,
    pressure,
    saturation,
    sat_history,
    storage,
    step_volume,
    transmiss,
    perf_cell,
    perf_index,
    control,
    target,
):
    vmem = pl.BlockSpec(memory_space=pltpu.VMEM)
    hbm = pl.BlockSpec(memory_space=pltpu.HBM)
    dma = pltpu.SemaphoreType.DMA
    block = (L, R, C)
    side = (4, 16, C)
    mid = pl.pallas_call(
        functools.partial(exchange, count_x, count_z),
        out_shape=[
            pltpu.VMEM(shape, F32)
            for shape in (
                block,
                (3, *block),
                block,
                (2, *block),
                (3, *block),
                *[block] * 6,
                *[side] * 3,
                (8, 1, C),
                (4, 1, C),
                *[(4, 48, C)] * 2,
                (4, 24, C),
                (4, 32, C),
                (4, 4, C),
                (1, WELLS),
            )
        ],
        in_specs=[hbm] * 10,
        out_specs=[vmem] * 22,
        scratch_shapes=[
            pltpu.VMEM(block, F32),
            pltpu.VMEM(block, F32),
            pltpu.VMEM((3, *block), F32),
            *[pltpu.VMEM(block, F32)] * 3,
            pltpu.VMEM(side, F32),
            pltpu.VMEM((L + 2, R, C), F32),
            pltpu.VMEM((2, L, C), F32),
            pltpu.VMEM((L + 2, R, C), F32),
            pltpu.VMEM((2, L, C), F32),
            pltpu.VMEM(((L + 2) * R, 512), BF16),
            pltpu.VMEM((C, 512), BF16),
            pltpu.VMEM((512, C), BF16),
            pltpu.VMEM((2, C, 512), BF16),
            *[pltpu.VMEM((4, 88, C), F32)] * 2,
            *[pltpu.VMEM((4, 5, C), F32)] * 2,
            pltpu.VMEM((4, 24, C), F32),
            pltpu.VMEM((4, 32, C), F32),
            pltpu.VMEM((4, 4, C), F32),
            *[pltpu.VMEM((2, 16, 128), F32)] * 2,
            pltpu.VMEM((1, 128), F32),
            pltpu.VMEM((12, 1, 128), F32),
            pltpu.VMEM((NP, WELLS), jnp.int32),
            pltpu.VMEM((NP, WELLS), F32),
            pltpu.VMEM((1, WELLS), jnp.int32),
            pltpu.VMEM((1, WELLS), F32),
            dma((19,)),
            dma((31,)),
        ],
        compiler_params=pltpu.CompilerParams(
            collective_id=0, has_side_effects=True, vmem_limit_bytes=VMEM_LIMIT
        ),
        name="exchange",
    )(
        *[
            pltpu.with_memory_space_constraint(values, pltpu.HBM)
            for values in (
                pressure,
                saturation,
                sat_history,
                storage,
                step_volume,
                transmiss,
                perf_cell.T,
                perf_index.T,
                control.reshape(1, WELLS),
                target.reshape(1, WELLS),
            )
        ]
    )
    *fields, hole = pl.pallas_call(
        solve,
        out_shape=[jax.ShapeDtypeStruct(block, F32)] * 4
        + [jax.ShapeDtypeStruct((1, WELLS), F32)],
        in_specs=[vmem] * 22,
        out_specs=[hbm] * 5,
        scratch_shapes=[
            pltpu.VMEM((4, 2, 16, C), F32),
            *[pltpu.VMEM(block, F32)] * 3,
            dma((3, 4)),
        ],
        compiler_params=pltpu.CompilerParams(vmem_limit_bytes=VMEM_LIMIT),
        name="solve",
    )(*mid)
    return (*fields, hole.reshape(WELLS))


def solution(mesh):
    cells = P("gz", "gx", None)
    return jax.shard_map(
        functools.partial(body, mesh.shape["gx"], mesh.shape["gz"]),
        mesh=mesh,
        in_specs=(
            *[cells] * 5,
            P(None, "gz", "gx", None),
            P("gx", None),
            P("gx", None),
            P("gx"),
            P("gx"),
        ),
        out_specs=(*[cells] * 4, P("gx")),
        check_vma=False,
    )
```
